32 devices in a mesh: row: 4 (over z), col: 8 (over y, x, core).
Axes of the slice: x: 2, y: 2, z: 4, core: 2. Of those that a mesh axis runs over, the one named last changes fastest.
Arguments:
- pair_products: bfloat16 [32, 64, 64, 64], P(('row', 'col')), may hold values from -6 to 6
- pw_index: int32 [8192], replicated, may hold values from 4096 to 131071, as said below
- valence_band: int32 [32], replicated, may hold values from 0 to 2047
- conduction_band: int32 [32], replicated, may hold values from 0 to 2047
- valence_energy: float32 [2048], replicated, may hold values from -10 to -0.5
- conduction_energy: float32 [2048], replicated, may hold values from 0.5 to 10
- imag_freq: float32 [2], replicated, may hold values from 0.3 to 12
Outputs:
- chi0: float32 [2, 16384, 16384], P(None, 'row', 'col')
The draws below stay inside these ranges and needn't reach their ends.
Inputs may be any that keep to these rules, and one draw needn't show every extreme that they name: `pw_index`: distinct flat indices (first grid index slowest) of grid points whose first component lies in 1 to 31, so no G-vector is zero and none is the negative of another.
All inputs are finite; a program needn't handle non-finite values.
Results may differ from the reference program's by a relative error of at most 0.0048.
Values may be sent and summed in bfloat16 or wider, within the bound.
A program may use at most 128 MiB of HBM per device.

```python
import math
import jax
import jax.numpy as jnp
from jax import lax

GRID = 64
NG = 8192
NFREQ = 2
NV = 2048
NC = 2048
PAIRS = 32


def draw_pw_index(key, part):
    plane = GRID * GRID
    count = (GRID // 2 - 1) * plane
    scores = jax.random.permutation(key, count)
    scores = scores.at[0].set(count).at[count - 1].set(count + 1)
    chosen = lax.top_k(scores, NG)[1]
    return ((1 + chosen // plane) * plane + chosen % plane).astype(jnp.int32)


def set_ends(entries, key, low, high):
    longest = entries.shape.index(max(entries.shape))
    spots = []
    for shift in (0, 1):
        where = [jax.random.randint(jax.random.fold_in(key, axis), (), 0, length) for axis, length in enumerate(entries.shape)]
        where[longest] = (where[longest] + shift) % entries.shape[longest]
        spots.append(tuple(where))
    return entries.at[spots[0]].set(low).at[spots[1]].set(high)


def steps_of(own_key, dims, cuts, low, largest):
    def one(dim, blocks):
        heights = jax.random.uniform(jax.random.fold_in(jax.random.fold_in(own_key, 6), dim), (blocks,), jnp.float32, low / len(cuts), largest / len(cuts))
        return jnp.repeat(jnp.exp(heights), dims[dim] // blocks).reshape((-1,) + (1,) * (len(dims) - dim - 1))

    loudness = one(*cuts[0])
    for cut in cuts[1:]:
        loudness = loudness * one(*cut)
    return loudness


def normal_values(stream_key, extent, width, limit, cuts=(), held_as=jnp.bfloat16):
    drawn = jax.random.normal(stream_key, extent, jnp.float32) * width
    if len(cuts) > 0:
        drawn = steps_of(stream_key, extent, cuts, -0.22, 0.18) * drawn
    return jnp.clip(drawn, min=-limit, max=limit).astype(held_as)


def setup_inputs(seed: int = 0) -> dict:
    key_of = jax.random.split(jax.random.key(seed), 8)
    pair_products = normal_values(key_of[0], (PAIRS, GRID, GRID, GRID), 1.0, 6.0, ((0, 32),))
    pw_index = draw_pw_index(jax.random.fold_in(key_of[7], 71), 0)
    valence_band = set_ends(jax.random.randint(key_of[2], (PAIRS,), 0, NV), jax.random.fold_in(key_of[2], 1), 0, NV - 1).astype(jnp.int32)
    conduction_band = set_ends(jax.random.randint(key_of[3], (PAIRS,), 0, NC), jax.random.fold_in(key_of[3], 1), 0, NC - 1).astype(jnp.int32)
    valence_energy = jnp.clip(jax.random.uniform(key_of[4], (NV,), jnp.float32, -10.0, -0.5), -10.0, -0.5)
    conduction_energy = jnp.clip(jax.random.uniform(key_of[5], (NC,), jnp.float32, 0.5, 10.0), 0.5, 10.0)
    imag_freq = jnp.clip(jnp.exp(jax.random.uniform(key_of[6], (NFREQ,), jnp.float32, math.log(0.3), math.log(12.0))), 0.3, 12.0)
    return dict(pair_products=pair_products, pw_index=pw_index, valence_band=valence_band, conduction_band=conduction_band, valence_energy=valence_energy, conduction_energy=conduction_energy, imag_freq=imag_freq)


def pair_weights(valence_band, conduction_band, valence_energy, conduction_energy, imag_freq):
    gap = conduction_energy[conduction_band] - valence_energy[valence_band]
    total = valence_band.shape[0]
    return -4.0 * gap[:, None] / (gap[:, None] ** 2 + imag_freq[None, :] ** 2) / jnp.sqrt(jnp.float32(total))

def reference(pair_products, pw_index, valence_band, conduction_band, valence_energy, conduction_energy, imag_freq):
    scale = float(GRID) ** (-1.5)

    def single(product):
        spectrum = jnp.fft.fftn(product.astype(jnp.float32)).reshape(-1)
        picked = spectrum[pw_index]
        return (jnp.concatenate([jnp.real(picked), -jnp.imag(picked)]) * scale).astype(jnp.bfloat16)
    coefficients = lax.map(single, pair_products)
    weights = pair_weights(valence_band, conduction_band, valence_energy, conduction_energy, imag_freq)
    left = coefficients.astype(jnp.float32)
    results = []
    for freq in range(NFREQ):
        weighted = (left * weights[:, freq:freq + 1]).astype(jnp.bfloat16).astype(jnp.float32)
        results.append(jnp.dot(left.T, weighted, preferred_element_type=jnp.float32))
    return jnp.stack(results)
```

```python
import math

import jax
import jax.numpy as jnp
import numpy as np
from jax import lax
from jax.experimental import pallas as pl
from jax.experimental.pallas import tpu as pltpu
from jax.sharding import PartitionSpec as P

MESH = pl.DeviceIdType.MESH
LANES = 128


def split(values):
    high = values.astype(jnp.bfloat16)
    low = (values - high.astype(jnp.float32)).astype(jnp.bfloat16)
    return high, low


def fourier_tables(points):
    counter = np.arange(points)
    angles = (counter[:, None] * counter[None, :] % points) * (2.0 * math.pi / points)
    cosine, sine = np.cos(angles), np.sin(angles)
    upper = points // 2

    def halves(table):
        single = table.astype(np.float32)
        high = single.astype(jnp.bfloat16)
        return high, (single - high.astype(np.float32)).astype(jnp.bfloat16)

    along_z = np.concatenate(halves(np.concatenate([cosine, -sine], axis=1)), axis=0)
    high, low = halves(np.concatenate([cosine, sine], axis=0))
    along_y = np.concatenate([high, high, low], axis=1)
    scale = float(points) ** (-1.5)
    high, low = halves(np.concatenate([cosine[:upper], sine[:upper]], axis=0) * scale)
    along_x = np.concatenate([high, high, low], axis=1)
    return [along_z, along_y, along_x]


def dot(left, right):
    return lax.dot_general(
        left, right, (((1,), (0,)), ((), ())), preferred_element_type=jnp.float32
    )


def column_of(row):
    size = row.shape[1]
    here = lax.broadcasted_iota(jnp.int32, (size, size), 0)
    there = lax.broadcasted_iota(jnp.int32, (size, size), 1)
    return jnp.sum(jnp.where(here == there, row, 0.0), axis=1, keepdims=True)


def lookup(indices, table):
    column = column_of(indices.astype(jnp.float32))
    slots = lax.broadcasted_iota(jnp.int32, (column.shape[0], table.shape[1]), 1)
    return jnp.sum(
        jnp.where(column == slots.astype(jnp.float32), table, 0.0), axis=1, keepdims=True
    )


def transform_kernel(
    x_ref, index_ref, z_ref, y_ref, x_table_ref,
    valence_band, conduction_band, valence_energy, conduction_energy, imag_freq,
    row_panel, col_panel, weights,
    planes, spectrum, picked, by_row, by_col,
    row_send, row_recv, col_send, col_recv,
    share_send, share_recv, pass_send, pass_recv,
):
    rows, cols, tall = row_panel.shape[:3]
    short = col_panel.shape[2]
    phases = row_send.shape[0]
    chunk_lines = tall // phases
    r, c = lax.axis_index("row"), lax.axis_index("col")

    def each(count, action):
        def body(step, carry):
            action(step)
            return carry

        lax.fori_loop(1, count, body, 0)

    def ahead(i):
        return lax.rem(r + i, rows)

    def behind(i):
        return lax.rem(r - i + rows, rows)

    def onward(k):
        return lax.rem(c + k, cols)

    def back(k):
        return lax.rem(c - k + cols, cols)

    def remote(source, target, send, recv, device):
        return pltpu.make_async_remote_copy(
            src_ref=source, dst_ref=target, send_sem=send, recv_sem=recv,
            device_id=device, device_id_type=MESH)

    def lines_of(phase):
        return pl.ds(phase * chunk_lines, chunk_lines)

    def row_copy(phase, i, source):
        return remote(
            by_row.at[ahead(i), lines_of(phase)], row_panel.at[source, c, lines_of(phase)],
            row_send.at[phase, i], row_recv.at[phase, i], (ahead(i), c))

    def col_copy(k, source):
        return remote(
            by_col.at[onward(k)], col_panel.at[r, source],
            col_send.at[k], col_recv.at[k], (r, onward(k)))

    def share(phase, i, k, held, source):
        return remote(
            held, row_panel.at[behind(i), source, lines_of(phase)],
            share_send.at[phase, i, k], share_recv.at[phase, i, k], (r, onward(k)))

    def hand_on(i, source):
        return remote(
            col_panel.at[r], col_panel.at[source],
            pass_send.at[i], pass_recv.at[i], (ahead(i), c))

    barrier = pltpu.get_barrier_semaphore()
    each(rows, lambda i: pl.semaphore_signal(
        barrier, inc=1, device_id=(ahead(i), c), device_id_type=MESH))
    each(cols, lambda k: pl.semaphore_signal(
        barrier, inc=1, device_id=(r, onward(k)), device_id_type=MESH))

    points = x_ref.shape[0]
    upper = points // 2
    wide = 2 * points
    step = min(16, points)
    along_z, along_y, along_x = z_ref[...], y_ref[...], x_table_ref[...]
    sign = jnp.where(lax.broadcasted_iota(jnp.int32, (points, wide), 1) < points, 1.0, -1.0)

    @pl.loop(0, points // step, unroll=points // step)
    def _(block):
        start = pl.multiple_of(block * step, step)
        data = x_ref[pl.ds(start, step)].reshape(step * points, points)
        lines = dot(jnp.concatenate([data, data], axis=1), along_z)
        high, low = split(lines)
        for pair in range(step // 2):
            blocks = []
            for side in range(2):
                rows = slice((2 * pair + side) * points, (2 * pair + side + 1) * points)
                blocks.append(jnp.concatenate([high[rows], low[rows], high[rows]], axis=0))
            result = dot(along_y, jnp.concatenate(blocks, axis=1))
            for side in range(2):
                part = result[:, side * wide:(side + 1) * wide]
                rows = pl.ds(pl.multiple_of((start + 2 * pair + side) * points, points), points)
                planes[rows, :] = part[:points] + sign * pltpu.roll(part[points:], points, 1)

    per_group = spectrum.shape[1] // LANES
    groups = points // 2 // per_group
    half_rows = groups * upper
    first_half = lax.broadcasted_iota(jnp.int32, (upper, wide), 1) < points

    for group in range(groups):

        @pl.loop(0, per_group, unroll=8)
        def _(place):
            base = 2 * (group * per_group + place)
            blocks = []
            for side in range(2):
                high, low = split(planes[pl.ds(base + side, points, stride=points), :])
                blocks.append(jnp.concatenate([high, low, high], axis=0))
            result = dot(along_x, jnp.concatenate(blocks, axis=1))
            even_cos, odd_cos = result[:upper, :wide], result[:upper, wide:]
            even_sin, odd_sin = result[upper:, :wide], result[upper:, wide:]

            def join(left, right, turn_left, turn_right):
                left = pltpu.roll(left, points, 1) if turn_left else left
                right = pltpu.roll(right, points, 1) if turn_right else right
                return jnp.where(first_half, left, right)

            real = join(even_cos, odd_cos, False, True) + join(even_sin, odd_sin, True, False)
            imag = join(even_sin, odd_sin, False, True) - join(even_cos, odd_cos, True, False)
            columns = pl.ds(pl.multiple_of(place * LANES, LANES), LANES)
            spectrum[group * upper:(group + 1) * upper, columns] = real.astype(jnp.bfloat16)
            spectrum[half_rows + group * upper:half_rows + (group + 1) * upper, columns] = (
                imag.astype(jnp.bfloat16)
            )

    depth = spectrum.shape[1]
    count = index_ref.shape[1]
    width = 256
    part = 256
    local = lax.broadcasted_iota(jnp.int32, (part, width), 0).astype(jnp.float32).astype(jnp.bfloat16)
    row_of = lax.broadcasted_iota(jnp.int32, (half_rows, width), 0)
    one = jnp.ones((part, width), jnp.bfloat16)
    zero = jnp.zeros((part, width), jnp.bfloat16)

    lines_per_step = width // LANES
    steps_per_block = chunk_lines // lines_per_step

    def select(phase, step):
        line = (step // steps_per_block) * tall + phase * chunk_lines
        line = line + (step % steps_per_block) * lines_per_step
        start = pl.multiple_of(line * LANES, width)
        index = index_ref[:, pl.ds(start, width)]
        column = index % depth
        upper_part = index // depth
        row = (upper_part % groups) * upper + upper_part // groups
        total = jnp.zeros((2 * half_rows, width), jnp.float32)
        for at in range(depth // part):
            shifted = (column - at * part).astype(jnp.float32).astype(jnp.bfloat16)
            chosen = jnp.where(local == jnp.broadcast_to(shifted, local.shape), one, zero)
            total = total + dot(spectrum[:, at * part:(at + 1) * part], chosen)
        mask = row_of == row
        real = jnp.sum(jnp.where(mask, total[:half_rows], 0.0), axis=0, keepdims=True)
        imag = jnp.sum(jnp.where(mask, total[half_rows:], 0.0), axis=0, keepdims=True)
        for side in range(lines_per_step):
            lanes = slice(side * LANES, (side + 1) * LANES)
            picked[pl.ds(line + side, 1), :] = real[:, lanes]
            picked[pl.ds(count // LANES + line + side, 1), :] = imag[:, lanes]

    def forward(phase):
        def one(i):
            source = behind(i)
            row_copy(phase, i, source).wait_recv()
            held = row_panel.at[source, c, lines_of(phase)]
            each(cols, lambda k: share(phase, i, k, held, c).start())

        each(rows, one)

    def phase_of(block):
        return lax.rem(block * short // chunk_lines, phases)

    def pass_columns():
        col_panel[r, c] = by_col[c]
        each(cols, lambda k: col_copy(k, back(k)).wait_recv())
        each(rows, lambda i: hand_on(i, r).start())

    for phase in range(phases):

        @pl.loop(0, rows // 2 * steps_per_block, unroll=8)
        def _(step):
            select(phase, step)

        for block in range(rows):
            first = block * tall + phase * chunk_lines
            values = picked[first:first + chunk_lines, :].astype(jnp.bfloat16)
            by_row[block, phase * chunk_lines:(phase + 1) * chunk_lines, :] = values
            for at in range(chunk_lines // short):
                by_col[first // short + at] = picked[
                    first + at * short:first + (at + 1) * short, :
                ].astype(jnp.bfloat16)
        if phase == 0:
            pl.semaphore_wait(barrier, rows + cols - 2)
        each(rows, lambda i: row_copy(phase, i, r).start())

        def send_col(k):
            @pl.when(phase_of(onward(k)) == phase)
            def _():
                col_copy(k, c).start()

        each(cols, send_col)
        if phase > 0:
            pl.when(phase_of(c) == phase - 1)(pass_columns)
        held = by_row.at[r, lines_of(phase)]
        each(cols, lambda k: share(phase, 0, k, held, c).start())
        if phase > 0:
            forward(phase - 1)

    row_panel[r, c] = by_row[r]
    pl.when(phase_of(c) == phases - 1)(pass_columns)
    forward(phases - 1)

    gap = lookup(conduction_band[...], conduction_energy[...]) - lookup(
        valence_band[...], valence_energy[...]
    )
    root = math.sqrt(gap.shape[0])
    for freq in range(weights.shape[1]):
        omega = imag_freq[:, freq:freq + 1]
        weights[:, freq:freq + 1] = -4.0 * gap / (gap * gap + omega * omega) / root

    each(cols, lambda k: col_copy(k, c).wait_send())

    def passed(i):
        hand_on(i, behind(i)).wait_recv()
        hand_on(i, r).wait_send()

    each(rows, passed)
    for phase in range(phases):
        each(rows, lambda i: row_copy(phase, i, r).wait_send())

        def finish(i, carry):
            held = row_panel.at[behind(i), c, lines_of(phase)]

            def ending(k):
                share(phase, i, k, held, back(k)).wait_recv()
                share(phase, i, k, held, c).wait_send()

            each(cols, ending)
            return carry

        lax.fori_loop(0, rows, finish, 0)


def transform(product, pw_index, row_count, col_count, *bands):
    bands = [values.reshape(1, -1) for values in bands]
    points = product.shape[0]
    count = pw_index.shape[0]
    lines = 2 * count // LANES
    tall, short = lines // row_count, lines // col_count
    phases = 2 if tall % 32 == 0 and (tall // 2) % short == 0 else 1
    tables = [jnp.asarray(table) for table in fourier_tables(points)]
    depth = 1024
    whole = pl.BlockSpec(memory_space=pltpu.VMEM)
    dma = pltpu.SemaphoreType.DMA
    return pl.pallas_call(
        transform_kernel,
        out_shape=(
            pltpu.VMEM((row_count, col_count, tall, LANES), jnp.bfloat16),
            pltpu.VMEM((row_count, col_count, short, LANES), jnp.bfloat16),
            pltpu.VMEM((bands[0].shape[1], bands[-1].shape[1]), jnp.float32),
        ),
        in_specs=[whole] * (2 + len(tables) + len(bands)),
        out_specs=(whole, whole, whole),
        scratch_shapes=[
            pltpu.VMEM((points * points, 2 * points), jnp.float32),
            pltpu.VMEM((points**3 // depth, depth), jnp.bfloat16),
            pltpu.VMEM((lines, LANES), jnp.float32),
            pltpu.VMEM((row_count, tall, LANES), jnp.bfloat16),
            pltpu.VMEM((col_count, short, LANES), jnp.bfloat16),
            dma((phases, row_count)), dma((phases, row_count)),
            dma((col_count,)), dma((col_count,)),
            dma((phases, row_count, col_count)), dma((phases, row_count, col_count)),
            dma((row_count,)), dma((row_count,)),
        ],
        compiler_params=pltpu.CompilerParams(collective_id=0, has_side_effects=True),
        name="spectrum",
    )(product, pw_index.reshape(1, count), *tables, *bands)


def product_kernel(row_ref, col_ref, weight_ref, out_ref, row_lines, col_lines, left, right, ring, sems):
    pairs = row_ref.shape[0]
    freq_count, row_width, _ = out_ref.shape
    slots, height = ring.shape[0], ring.shape[1]

    for ref, lines, is_left in ((row_ref, row_lines, True), (col_ref, col_lines, False)):
        if len(ref.shape) == 3:
            blocks = ref.shape[1]
            lines[...] = ref[...].astype(jnp.float32).reshape(lines.shape)
        else:
            blocks = ref.shape[1] // LANES
        for block in range(0 if is_left else blocks):
            lanes = slice(block * LANES, (block + 1) * LANES)
            if len(ref.shape) == 3:
                values = lines[pl.ds(block, pairs, stride=blocks), :]
            else:
                values = ref[:, lanes].astype(jnp.float32)
            if not is_left:
                for freq in range(freq_count):
                    right[freq, :, lanes] = (
                        values * weight_ref[:, freq:freq + 1]
                    ).astype(jnp.bfloat16)

    steps = row_width // height

    def write(slot, freq, step):
        rows = pl.ds(pl.multiple_of(step * height, height), height)
        return pltpu.make_async_copy(ring.at[slot], out_ref.at[freq, rows], sems.at[slot])

    @pl.loop(0, steps)
    def _(step):
        for part in range(height // LANES):
            block = step * (height // LANES) + part
            if len(row_ref.shape) == 3:
                values = row_lines[pl.ds(block, pairs, stride=row_ref.shape[1]), :]
            else:
                values = row_ref[:, pl.ds(pl.multiple_of(block * LANES, LANES), LANES)]
                values = values.astype(jnp.float32)
            left[part * LANES:(part + 1) * LANES, :] = values.T.astype(jnp.bfloat16)
        panel = left[...]
        for freq in range(freq_count):
            unit = step * freq_count + freq
            slot = lax.rem(unit, slots)

            @pl.when(unit >= slots)
            def _():
                write(slot, freq, step).wait()

            ring[slot] = dot(panel, right[freq])
            write(slot, freq, step).start()

    for slot in range(min(slots, steps * freq_count)):
        write(slot, 0, 0).wait()


def product(row_panel, col_panel, weights):
    pairs, freq_count = weights.shape
    row_width = row_panel.shape[2] * LANES
    col_width = col_panel.shape[2] * LANES
    panels = []
    lines = []
    for panel in (row_panel, col_panel):
        height = panel.shape[2]
        if height % 16 == 0:
            panels.append(pltpu.with_memory_space_constraint(panel.reshape(pairs, height, LANES), pltpu.VMEM))
            lines.append(pltpu.VMEM((pairs * height, LANES), jnp.float32))
        else:
            panels.append(panel.reshape(pairs, height * LANES))
            lines.append(pltpu.VMEM((8, LANES), jnp.float32))
    block = min(256, row_width)
    slots = 4
    whole = pl.BlockSpec(memory_space=pltpu.VMEM)
    return pl.pallas_call(
        product_kernel,
        out_shape=jax.ShapeDtypeStruct((freq_count, row_width, col_width), jnp.float32),
        in_specs=[whole, whole, whole],
        out_specs=pl.BlockSpec(memory_space=pl.ANY),
        scratch_shapes=lines + [
            pltpu.VMEM((block, pairs), jnp.bfloat16),
            pltpu.VMEM((freq_count, pairs, col_width), jnp.bfloat16),
            pltpu.VMEM((slots, block, col_width), jnp.float32),
            pltpu.SemaphoreType.DMA((slots,)),
        ],
        name="product",
    )(*panels, pltpu.with_memory_space_constraint(weights, pltpu.VMEM))


def shards(
    pair_products,
    pw_index,
    valence_band,
    conduction_band,
    valence_energy,
    conduction_energy,
    imag_freq,
):
    rows, cols = lax.axis_size("row"), lax.axis_size("col")
    row_panel, col_panel, weights = transform(
        pair_products[0], pw_index, rows, cols,
        valence_band, conduction_band, valence_energy, conduction_energy, imag_freq,
    )
    return product(row_panel, col_panel, weights)


def solution(mesh):
    in_specs = (P(("row", "col"), None, None, None), P(), P(), P(), P(), P(), P())
    out_specs = P(None, "row", "col")
    return jax.shard_map(shards, mesh=mesh, in_specs=in_specs, out_specs=out_specs, check_vma=False)
```

```python
import math

import jax
import jax.numpy as jnp
import numpy as np
from jax import lax
from jax.experimental import pallas as pl
from jax.experimental.pallas import tpu as pltpu
from jax.sharding import PartitionSpec as P

MESH = pl.DeviceIdType.MESH
LANES = 128


def split(values):
    high = values.astype(jnp.bfloat16)
    low = (values - high.astype(jnp.float32)).astype(jnp.bfloat16)
    return high, low


def fourier_tables(points):
    counter = np.arange(points)
    angles = (counter[:, None] * counter[None, :] % points) * (2.0 * math.pi / points)
    cosine, sine = np.cos(angles), np.sin(angles)
    upper = points // 2

    def halves(table):
        single = table.astype(np.float32)
        high = single.astype(jnp.bfloat16)
        return high, (single - high.astype(np.float32)).astype(jnp.bfloat16)

    along_z = np.concatenate(halves(np.concatenate([cosine, -sine], axis=1)), axis=0)
    high, low = halves(np.concatenate([cosine, sine], axis=0))
    along_y = np.concatenate([high, high, low], axis=1)
    scale = float(points) ** (-1.5)
    high, low = halves(np.concatenate([cosine[:upper], sine[:upper]], axis=0) * scale)
    along_x = np.concatenate([high, high, low], axis=1)
    return [along_z, along_y, along_x]


def dot(left, right):
    return lax.dot_general(
        left, right, (((1,), (0,)), ((), ())), preferred_element_type=jnp.float32
    )


def column_of(row):
    size = row.shape[1]
    here = lax.broadcasted_iota(jnp.int32, (size, size), 0)
    there = lax.broadcasted_iota(jnp.int32, (size, size), 1)
    return jnp.sum(jnp.where(here == there, row, 0.0), axis=1, keepdims=True)


def lookup(indices, table):
    column = column_of(indices.astype(jnp.float32))
    slots = lax.broadcasted_iota(jnp.int32, (column.shape[0], table.shape[1]), 1)
    return jnp.sum(
        jnp.where(column == slots.astype(jnp.float32), table, 0.0), axis=1, keepdims=True
    )


def transform_kernel(
    x_hbm, index_hbm, z_hbm, y_hbm, x_table_hbm,
    valence_band_hbm, conduction_band_hbm, valence_energy_hbm, conduction_energy_hbm, imag_freq_hbm,
    row_panel, col_panel, weights,
    x_ref, index_ref, z_ref, y_ref, x_table_ref,
    valence_band, conduction_band, valence_energy, conduction_energy, imag_freq,
    planes, spectrum, picked, staged,
    loaded, chunk_loaded, row_send, row_recv, col_send, col_recv,
):
    cols, short = staged.shape[:2]
    per_row = row_panel.shape[1]
    rows = cols // per_row
    pairs = rows * cols
    phases = cols // 2
    r, c = lax.axis_index("row"), lax.axis_index("col")

    points = x_ref.shape[0]
    upper = points // 2
    wide = 2 * points
    step = min(16, points)
    chunks = points // step

    def chunk(at):
        planes_of = pl.ds(at * step, step)
        return pltpu.make_async_copy(x_hbm.at[planes_of], x_ref.at[planes_of], chunk_loaded.at[at])

    operands = [
        (z_hbm, z_ref), (y_hbm, y_ref), (x_table_hbm, x_table_ref), (index_hbm, index_ref),
        (valence_band_hbm, valence_band), (conduction_band_hbm, conduction_band),
        (valence_energy_hbm, valence_energy), (conduction_energy_hbm, conduction_energy),
        (imag_freq_hbm, imag_freq),
    ]

    def load(at):
        source, target = operands[at]
        return pltpu.make_async_copy(source, target, loaded.at[at])

    load(0).start()
    chunk(0).start()
    load(1).start()
    for at in range(1, chunks):
        chunk(at).start()
    for at in range(2, len(operands)):
        load(at).start()

    def ahead(i):
        return lax.rem(r + i, rows)

    def onward(k):
        return lax.rem(c + k, cols)

    def loop(first, last, action):
        def body(at, carry):
            action(at)
            return carry

        lax.fori_loop(first, last, body, 0)

    barrier = pltpu.get_barrier_semaphore()

    def greet(at):
        pl.semaphore_signal(
            barrier, inc=1, device_id=(ahead(at // cols), onward(lax.rem(at, cols))),
            device_id_type=MESH)

    loop(1, pairs, greet)

    load(0).wait()
    load(1).wait()
    along_z, along_y = z_ref[...], y_ref[...]
    sign = jnp.where(lax.broadcasted_iota(jnp.int32, (points, wide), 1) < points, 1.0, -1.0)

    for at in range(chunks):
        chunk(at).wait()
        start = at * step
        data = x_ref[start:start + step].reshape(step * points, points)
        lines = dot(jnp.concatenate([data, data], axis=1), along_z)
        high, low = split(lines)
        for pair in range(step // 2):
            blocks = []
            for side in range(2):
                lot = slice((2 * pair + side) * points, (2 * pair + side + 1) * points)
                blocks.append(jnp.concatenate([high[lot], low[lot], high[lot]], axis=0))
            result = dot(along_y, jnp.concatenate(blocks, axis=1))
            for side in range(2):
                part = result[:, side * wide:(side + 1) * wide]
                first = (start + 2 * pair + side) * points
                planes[first:first + points, :] = (
                    part[:points] + sign * pltpu.roll(part[points:], points, 1)
                )

    load(2).wait()
    along_x = x_table_ref[...]
    per_group = spectrum.shape[1] // LANES
    groups = points // 2 // per_group
    half_rows = groups * upper
    first_half = lax.broadcasted_iota(jnp.int32, (upper, wide), 1) < points

    for group in range(groups):

        @pl.loop(0, per_group, unroll=8)
        def _(place):
            base = 2 * (group * per_group + place)
            blocks = []
            for side in range(2):
                high, low = split(planes[pl.ds(base + side, points, stride=points), :])
                blocks.append(jnp.concatenate([high, low, high], axis=0))
            result = dot(along_x, jnp.concatenate(blocks, axis=1))
            even_cos, odd_cos = result[:upper, :wide], result[:upper, wide:]
            even_sin, odd_sin = result[upper:, :wide], result[upper:, wide:]

            def join(left, right, turn_left, turn_right):
                left = pltpu.roll(left, points, 1) if turn_left else left
                right = pltpu.roll(right, points, 1) if turn_right else right
                return jnp.where(first_half, left, right)

            real = join(even_cos, odd_cos, False, True) + join(even_sin, odd_sin, True, False)
            imag = join(even_sin, odd_sin, False, True) - join(even_cos, odd_cos, True, False)
            columns = pl.ds(pl.multiple_of(place * LANES, LANES), LANES)
            spectrum[group * upper:(group + 1) * upper, columns] = real.astype(jnp.bfloat16)
            spectrum[half_rows + group * upper:half_rows + (group + 1) * upper, columns] = (
                imag.astype(jnp.bfloat16)
            )

    depth = spectrum.shape[1]
    width = 256
    part = 256
    local = lax.broadcasted_iota(jnp.int32, (part, width), 0).astype(jnp.float32).astype(jnp.bfloat16)
    row_of = lax.broadcasted_iota(jnp.int32, (half_rows, width), 0)
    one = jnp.ones((part, width), jnp.bfloat16)
    zero = jnp.zeros((part, width), jnp.bfloat16)

    lines_per_step = width // LANES
    steps = short // lines_per_step
    load(3).wait()

    def select(own, step):
        line = step * lines_per_step
        start = pl.multiple_of((own * short + line) * LANES, width)
        index = index_ref[:, pl.ds(start, width)]
        column = index % depth
        upper_part = index // depth
        row = (upper_part % groups) * upper + upper_part // groups
        total = jnp.zeros((2 * half_rows, width), jnp.float32)
        for at in range(depth // part):
            shifted = (column - at * part).astype(jnp.float32).astype(jnp.bfloat16)
            chosen = jnp.where(local == jnp.broadcast_to(shifted, local.shape), one, zero)
            total = total + dot(spectrum[:, at * part:(at + 1) * part], chosen)
        mask = row_of == row
        real = jnp.sum(jnp.where(mask, total[:half_rows], 0.0), axis=0, keepdims=True)
        imag = jnp.sum(jnp.where(mask, total[half_rows:], 0.0), axis=0, keepdims=True)
        for side in range(lines_per_step):
            lanes = slice(side * LANES, (side + 1) * LANES)
            picked[pl.ds(line + side, 1), :] = real[:, lanes]
            picked[pl.ds(short + line + side, 1), :] = imag[:, lanes]

    def row_copy(own, k):
        lot = lax.rem(own, per_row)
        return pltpu.make_async_remote_copy(
            src_ref=staged.at[own], dst_ref=row_panel.at[r * cols + c, lot],
            send_sem=row_send, recv_sem=row_recv,
            device_id=(own // per_row, onward(k)), device_id_type=MESH)

    def col_copy(own, i):
        return pltpu.make_async_remote_copy(
            src_ref=staged.at[own], dst_ref=col_panel.at[r * cols + c],
            send_sem=col_send, recv_sem=col_recv,
            device_id=(ahead(i), own), device_id_type=MESH)

    def distribute(own):
        inside = own // per_row == r
        loop(1, cols, lambda k: row_copy(own, k).start())
        loop(1, rows, lambda i: col_copy(own, i).start())

        @pl.when(own != c)
        def _():
            col_copy(own, 0).start()

        @pl.when(jnp.logical_not(inside))
        def _():
            row_copy(own, 0).start()

        @pl.when(inside)
        def _():
            row_panel[r * cols + c, lax.rem(own, per_row)] = staged[own]

        @pl.when(own == c)
        def _():
            col_panel[r * cols + c] = staged[own]

    turn = jnp.where(r < rows // 2, phases // 2, 0)
    for phase in range(phases):
        own = lax.rem(phase + turn, phases)

        @pl.loop(0, steps, unroll=min(8, steps))
        def _(step):
            select(own, step)

        for side in range(2):
            staged[own + side * phases] = picked[side * short:(side + 1) * short, :].astype(jnp.bfloat16)
        if phase == 0:
            pl.semaphore_wait(barrier, pairs - 1)
        for side in range(2):
            distribute(own + side * phases)

    for at in range(4, len(operands)):
        load(at).wait()
    gap = lookup(conduction_band[...], conduction_energy[...]) - lookup(
        valence_band[...], valence_energy[...]
    )
    root = math.sqrt(gap.shape[0])
    for freq in range(weights.shape[1]):
        omega = imag_freq[:, freq:freq + 1]
        weights[:, freq:freq + 1] = -4.0 * gap / (gap * gap + omega * omega) / root

    others = pl.ds(0, pairs - 1)
    for panel, sent, received in ((row_panel, row_send, row_recv), (col_panel, col_send, col_recv)):
        pltpu.make_async_copy(panel.at[others], panel.at[others], received).wait()
        pltpu.make_async_copy(panel.at[others], panel.at[others], sent).wait()


def transform(product, pw_index, row_count, col_count, *bands):
    bands = [values.reshape(1, -1) for values in bands]
    points = product.shape[0]
    count = pw_index.shape[0]
    pairs = row_count * col_count
    lines = 2 * count // LANES
    tall, short = lines // row_count, lines // col_count
    tables = [jnp.asarray(table) for table in fourier_tables(points)]
    depth = 1024
    dma = pltpu.SemaphoreType.DMA
    operands = [product, pw_index.reshape(1, count), *tables, *bands]
    operands = [pltpu.with_memory_space_constraint(value, pltpu.HBM) for value in operands]
    return pl.pallas_call(
        transform_kernel,
        out_shape=(
            pltpu.VMEM((pairs, tall // short, short, LANES), jnp.bfloat16),
            pltpu.VMEM((pairs, short, LANES), jnp.bfloat16),
            pltpu.VMEM((bands[0].shape[1], bands[-1].shape[1]), jnp.float32),
        ),
        in_specs=[pl.BlockSpec(memory_space=pltpu.HBM)] * len(operands),
        out_specs=(pl.BlockSpec(memory_space=pltpu.VMEM),) * 3,
        scratch_shapes=[pltpu.VMEM(value.shape, value.dtype) for value in operands] + [
            pltpu.VMEM((points * points, 2 * points), jnp.float32),
            pltpu.VMEM((points**3 // depth, depth), jnp.bfloat16),
            pltpu.VMEM((2 * short, LANES), jnp.float32),
            pltpu.VMEM((col_count, short, LANES), jnp.bfloat16),
            dma((len(operands) - 1,)), dma((points // min(16, points),)),
            dma, dma, dma, dma,
        ],
        compiler_params=pltpu.CompilerParams(collective_id=0, has_side_effects=True),
        name="spectrum",
    )(*operands)


def product_kernel(row_ref, col_ref, weight_ref, out_ref, row_lines, col_lines, left, right, ring, sems):
    pairs = row_ref.shape[0]
    freq_count, row_width, _ = out_ref.shape
    slots, height = ring.shape[0], ring.shape[1]

    for ref, lines, is_left in ((row_ref, row_lines, True), (col_ref, col_lines, False)):
        if len(ref.shape) == 3:
            blocks = ref.shape[1]
            lines[...] = ref[...].astype(jnp.float32).reshape(lines.shape)
        else:
            blocks = ref.shape[1] // LANES
        for block in range(0 if is_left else blocks):
            lanes = slice(block * LANES, (block + 1) * LANES)
            if len(ref.shape) == 3:
                values = lines[pl.ds(block, pairs, stride=blocks), :]
            else:
                values = ref[:, lanes].astype(jnp.float32)
            if not is_left:
                for freq in range(freq_count):
                    right[freq, :, lanes] = (
                        values * weight_ref[:, freq:freq + 1]
                    ).astype(jnp.bfloat16)

    steps = row_width // height

    def write(slot, freq, step):
        rows = pl.ds(pl.multiple_of(step * height, height), height)
        return pltpu.make_async_copy(ring.at[slot], out_ref.at[freq, rows], sems.at[slot])

    @pl.loop(0, steps)
    def _(step):
        for part in range(height // LANES):
            block = step * (height // LANES) + part
            if len(row_ref.shape) == 3:
                values = row_lines[pl.ds(block, pairs, stride=row_ref.shape[1]), :]
            else:
                values = row_ref[:, pl.ds(pl.multiple_of(block * LANES, LANES), LANES)]
                values = values.astype(jnp.float32)
            left[part * LANES:(part + 1) * LANES, :] = values.T.astype(jnp.bfloat16)
        panel = left[...]
        for freq in range(freq_count):
            unit = step * freq_count + freq
            slot = lax.rem(unit, slots)

            @pl.when(unit >= slots)
            def _():
                write(slot, freq, step).wait()

            ring[slot] = dot(panel, right[freq])
            write(slot, freq, step).start()

    for slot in range(min(slots, steps * freq_count)):
        write(slot, 0, 0).wait()


def product(row_panel, col_panel, weights):
    pairs, freq_count = weights.shape
    row_panel = row_panel.reshape(pairs, -1, LANES)
    row_width = row_panel.shape[1] * LANES
    col_width = col_panel.shape[1] * LANES
    panels = []
    lines = []
    for panel in (row_panel, col_panel):
        height = panel.shape[1]
        if height % 16 == 0:
            panels.append(pltpu.with_memory_space_constraint(panel, pltpu.VMEM))
            lines.append(pltpu.VMEM((pairs * height, LANES), jnp.float32))
        else:
            panels.append(panel.reshape(pairs, height * LANES))
            lines.append(pltpu.VMEM((8, LANES), jnp.float32))
    block = min(256, row_width)
    slots = 4
    whole = pl.BlockSpec(memory_space=pltpu.VMEM)
    return pl.pallas_call(
        product_kernel,
        out_shape=jax.ShapeDtypeStruct((freq_count, row_width, col_width), jnp.float32),
        in_specs=[whole, whole, whole],
        out_specs=pl.BlockSpec(memory_space=pl.ANY),
        scratch_shapes=lines + [
            pltpu.VMEM((block, pairs), jnp.bfloat16),
            pltpu.VMEM((freq_count, pairs, col_width), jnp.bfloat16),
            pltpu.VMEM((slots, block, col_width), jnp.float32),
            pltpu.SemaphoreType.DMA((slots,)),
        ],
        name="product",
    )(*panels, pltpu.with_memory_space_constraint(weights, pltpu.VMEM))


def shards(
    pair_products,
    pw_index,
    valence_band,
    conduction_band,
    valence_energy,
    conduction_energy,
    imag_freq,
):
    rows, cols = lax.axis_size("row"), lax.axis_size("col")
    row_panel, col_panel, weights = transform(
        pair_products[0], pw_index, rows, cols,
        valence_band, conduction_band, valence_energy, conduction_energy, imag_freq,
    )
    return product(row_panel, col_panel, weights)


def solution(mesh):
    in_specs = (P(("row", "col"), None, None, None), P(), P(), P(), P(), P(), P())
    out_specs = P(None, "row", "col")
    return jax.shard_map(shards, mesh=mesh, in_specs=in_specs, out_specs=out_specs, check_vma=False)
```

```python
import functools
import math

import jax
import jax.numpy as jnp
import numpy as np
from jax import lax
from jax.experimental import pallas as pl
from jax.experimental.pallas import tpu as pltpu
from jax.sharding import PartitionSpec as P

MESH = pl.DeviceIdType.MESH
LANES = 128


def split(values):
    high = values.astype(jnp.bfloat16)
    low = (values - high.astype(jnp.float32)).astype(jnp.bfloat16)
    return high, low


def fourier_tables(points):
    counter = np.arange(points)
    angles = (counter[:, None] * counter[None, :] % points) * (2.0 * math.pi / points)
    cosine, sine = np.cos(angles), np.sin(angles)
    upper = points // 2

    def halves(table):
        single = table.astype(np.float32)
        high = single.astype(jnp.bfloat16)
        return high, (single - high.astype(np.float32)).astype(jnp.bfloat16)

    along_z = np.concatenate(halves(np.concatenate([cosine, -sine], axis=1)), axis=0)
    high, low = halves(np.concatenate([cosine, sine], axis=0))
    along_y = np.concatenate([high, high, low], axis=1)
    scale = float(points) ** (-1.5)
    high, low = halves(np.concatenate([cosine[:upper], sine[:upper]], axis=0) * scale)
    along_x = np.concatenate([high, high, low], axis=1)
    return [along_z, along_y, along_x]


def dot(left, right):
    return lax.dot_general(
        left, right, (((1,), (0,)), ((), ())), preferred_element_type=jnp.float32
    )


def column_of(row):
    size = row.shape[1]
    here = lax.broadcasted_iota(jnp.int32, (size, size), 0)
    there = lax.broadcasted_iota(jnp.int32, (size, size), 1)
    return jnp.sum(jnp.where(here == there, row, 0.0), axis=1, keepdims=True)


def lookup(indices, table):
    column = column_of(indices.astype(jnp.float32))
    slots = lax.broadcasted_iota(jnp.int32, (column.shape[0], table.shape[1]), 1)
    return jnp.sum(
        jnp.where(column == slots.astype(jnp.float32), table, 0.0), axis=1, keepdims=True
    )


def transform_kernel(
    direct_last, x_hbm, index_hbm, z_hbm, y_hbm, x_table_hbm,
    valence_band_hbm, conduction_band_hbm, valence_energy_hbm, conduction_energy_hbm, imag_freq_hbm,
    row_panel, col_panel, weights,
    x_ref, index_ref, z_ref, y_ref, x_table_ref,
    valence_band, conduction_band, valence_energy, conduction_energy, imag_freq,
    planes, spectrum, picked, staged,
    loaded, chunk_loaded, row_send, row_recv, col_send, col_recv, across_send, across_recv,
):
    cols, short = staged.shape[:2]
    per_row = row_panel.shape[1]
    rows = cols // per_row
    pairs = rows * cols
    phases = cols // 2
    r, c = lax.axis_index("row"), lax.axis_index("col")

    points = x_ref.shape[0]
    upper = points // 2
    wide = 2 * points
    step = min(16, points)
    chunks = points // step

    def chunk(at):
        planes_of = pl.ds(at * step, step)
        return pltpu.make_async_copy(x_hbm.at[planes_of], x_ref.at[planes_of], chunk_loaded.at[at])

    operands = [
        (z_hbm, z_ref), (y_hbm, y_ref), (x_table_hbm, x_table_ref), (index_hbm, index_ref),
        (valence_band_hbm, valence_band), (conduction_band_hbm, conduction_band),
        (valence_energy_hbm, valence_energy), (conduction_energy_hbm, conduction_energy),
        (imag_freq_hbm, imag_freq),
    ]

    def load(at):
        source, target = operands[at]
        return pltpu.make_async_copy(source, target, loaded.at[at])

    load(0).start()
    chunk(0).start()
    load(1).start()
    for at in range(1, chunks):
        chunk(at).start()
    for at in range(2, len(operands)):
        load(at).start()

    def ahead(i):
        return lax.rem(r + i, rows)

    def onward(k):
        return lax.rem(c + k, cols)

    def loop(first, last, action):
        def body(at, carry):
            action(at)
            return carry

        lax.fori_loop(first, last, body, 0, unroll=last - first <= 8)

    barrier = pltpu.get_barrier_semaphore()

    def greet(at):
        pl.semaphore_signal(
            barrier, inc=1, device_id=(ahead(at // cols), onward(lax.rem(at, cols))),
            device_id_type=MESH)

    loop(1, pairs, greet)

    load(0).wait()
    load(1).wait()
    along_z, along_y = z_ref[...], y_ref[...]
    sign = jnp.where(lax.broadcasted_iota(jnp.int32, (points, wide), 1) < points, 1.0, -1.0)

    for at in range(chunks):
        chunk(at).wait()
        start = at * step
        data = x_ref[start:start + step].reshape(step * points, points)
        lines = dot(jnp.concatenate([data, data], axis=1), along_z)
        high, low = split(lines)
        for pair in range(step // 2):
            blocks = []
            for side in range(2):
                lot = slice((2 * pair + side) * points, (2 * pair + side + 1) * points)
                blocks.append(jnp.concatenate([high[lot], low[lot], high[lot]], axis=0))
            result = dot(along_y, jnp.concatenate(blocks, axis=1))
            for side in range(2):
                part = result[:, side * wide:(side + 1) * wide]
                first = (start + 2 * pair + side) * points
                planes[first:first + points, :] = (
                    part[:points] + sign * pltpu.roll(part[points:], points, 1)
                )

    load(2).wait()
    along_x = x_table_ref[...]
    per_group = spectrum.shape[1] // LANES
    groups = points // 2 // per_group
    half_rows = groups * upper
    first_half = lax.broadcasted_iota(jnp.int32, (upper, wide), 1) < points

    for group in range(groups):

        @pl.loop(0, per_group, unroll=8)
        def _(place):
            base = 2 * (group * per_group + place)
            blocks = []
            for side in range(2):
                high, low = split(planes[pl.ds(base + side, points, stride=points), :])
                blocks.append(jnp.concatenate([high, low, high], axis=0))
            result = dot(along_x, jnp.concatenate(blocks, axis=1))
            even_cos, odd_cos = result[:upper, :wide], result[:upper, wide:]
            even_sin, odd_sin = result[upper:, :wide], result[upper:, wide:]

            def join(left, right, turn_left, turn_right):
                left = pltpu.roll(left, points, 1) if turn_left else left
                right = pltpu.roll(right, points, 1) if turn_right else right
                return jnp.where(first_half, left, right)

            real = join(even_cos, odd_cos, False, True) + join(even_sin, odd_sin, True, False)
            imag = join(even_sin, odd_sin, False, True) - join(even_cos, odd_cos, True, False)
            columns = pl.ds(pl.multiple_of(place * LANES, LANES), LANES)
            spectrum[group * upper:(group + 1) * upper, columns] = real.astype(jnp.bfloat16)
            spectrum[half_rows + group * upper:half_rows + (group + 1) * upper, columns] = (
                imag.astype(jnp.bfloat16)
            )

    depth = spectrum.shape[1]
    width = 256
    part = 256
    local = lax.broadcasted_iota(jnp.int32, (part, width), 0).astype(jnp.float32).astype(jnp.bfloat16)
    row_of = lax.broadcasted_iota(jnp.int32, (half_rows, width), 0)
    one = jnp.ones((part, width), jnp.bfloat16)
    zero = jnp.zeros((part, width), jnp.bfloat16)

    lines_per_step = width // LANES
    steps = short // lines_per_step
    load(3).wait()

    def select(own, step):
        line = step * lines_per_step
        start = pl.multiple_of((own * short + line) * LANES, width)
        index = index_ref[:, pl.ds(start, width)]
        column = index % depth
        upper_part = index // depth
        row = (upper_part % groups) * upper + upper_part // groups
        total = jnp.zeros((2 * half_rows, width), jnp.float32)
        for at in range(depth // part):
            shifted = (column - at * part).astype(jnp.float32).astype(jnp.bfloat16)
            chosen = jnp.where(local == jnp.broadcast_to(shifted, local.shape), one, zero)
            total = total + dot(spectrum[:, at * part:(at + 1) * part], chosen)
        mask = row_of == row
        real = jnp.sum(jnp.where(mask, total[:half_rows], 0.0), axis=0, keepdims=True)
        imag = jnp.sum(jnp.where(mask, total[half_rows:], 0.0), axis=0, keepdims=True)
        for side in range(lines_per_step):
            lanes = slice(side * LANES, (side + 1) * LANES)
            picked[pl.ds(line + side, 1), :] = real[:, lanes]
            picked[pl.ds(short + line + side, 1), :] = imag[:, lanes]

    def row_copy(own, k):
        return pltpu.make_async_remote_copy(
            src_ref=staged.at[own], dst_ref=row_panel.at[r * cols + c, lax.rem(own, per_row)],
            send_sem=row_send, recv_sem=row_recv,
            device_id=(own // per_row, onward(k)), device_id_type=MESH)

    parity = lax.rem(c, 2)

    def across(own, at):
        lot = lax.rem(own, per_row)
        return pltpu.make_async_remote_copy(
            src_ref=staged.at[own], dst_ref=row_panel.at[r * cols + c, lot],
            send_sem=across_send, recv_sem=across_recv.at[r, c // 2, lot],
            device_id=(own // per_row, 2 * at + parity), device_id_type=MESH)

    def other_core(own, at):
        return pltpu.make_async_remote_copy(
            src_ref=staged.at[own], dst_ref=row_panel.at[r * cols + c, lax.rem(own, per_row)],
            send_sem=row_send, recv_sem=row_recv,
            device_id=(own // per_row, 2 * at + 1 - parity), device_id_type=MESH)

    def pass_on(held):
        return pltpu.make_async_remote_copy(
            src_ref=held, dst_ref=held, send_sem=row_send, recv_sem=row_recv,
            device_id=(r, c + 1 - 2 * parity), device_id_type=MESH)

    def col_copy(own, i):
        return pltpu.make_async_remote_copy(
            src_ref=staged.at[own], dst_ref=col_panel.at[r * cols + c],
            send_sem=col_send, recv_sem=col_recv,
            device_id=(ahead(i), own), device_id_type=MESH)

    def is_direct(phase):
        return direct_last and phase == phases - 1

    def distribute(own, phase):
        inside = own // per_row == r

        @pl.when(jnp.logical_not(inside))
        def _():
            loop(0, cols // 2, lambda at: across(own, at).start())
            if is_direct(phase):
                loop(0, cols // 2, lambda at: other_core(own, at).start())

        @pl.when(inside)
        def _():
            loop(1, cols, lambda k: row_copy(own, k).start())

        loop(1, rows, lambda i: col_copy(own, i).start())

        @pl.when(own != c)
        def _():
            col_copy(own, 0).start()

        @pl.when(inside)
        def _():
            row_panel[r * cols + c, lax.rem(own, per_row)] = staged[own]

        @pl.when(own == c)
        def _():
            col_panel[r * cols + c] = staged[own]

    def turn_of(row):
        return jnp.where(row < rows // 2, phases // 2, 0)

    def relay(phase, which):
        def one(i):
            source = ahead(i)
            own = lax.rem(phase + turn_of(source), phases)
            for side in range(2):
                group = own + side * phases
                mine = group // per_row == r
                if which == "early":
                    mine = jnp.logical_and(mine, source < r)
                elif which == "late":
                    mine = jnp.logical_and(mine, source > r)

                @pl.when(mine)
                def _():
                    lot = lax.rem(group, per_row)

                    def take(at):
                        held = row_panel.at[source * cols + 2 * at + parity, lot]
                        pltpu.make_async_copy(held, held, across_recv.at[source, at, lot]).wait()
                        if not is_direct(phase):
                            pass_on(held).start()

                    loop(0, cols // 2, take)

        loop(1, rows, one)

    for phase in range(phases):
        own = lax.rem(phase + turn_of(r), phases)

        @pl.loop(0, steps, unroll=min(8, steps))
        def _(step):
            select(own, step)

        for side in range(2):
            staged[own + side * phases] = picked[side * short:(side + 1) * short, :].astype(jnp.bfloat16)
        if phase == 0:
            pl.semaphore_wait(barrier, pairs - 1)
        for side in range(2):
            distribute(own + side * phases, phase)
        if phase >= 2:
            relay(phase - 2, "early")

    for at in range(4, len(operands)):
        load(at).wait()
    gap = lookup(conduction_band[...], conduction_energy[...]) - lookup(
        valence_band[...], valence_energy[...]
    )
    root = math.sqrt(gap.shape[0])
    for freq in range(weights.shape[1]):
        omega = imag_freq[:, freq:freq + 1]
        weights[:, freq:freq + 1] = -4.0 * gap / (gap * gap + omega * omega) / root

    for phase in range(phases):
        relay(phase, "late" if phase < phases - 2 else "all")

    for panel, count, sent, received in (
        (row_panel, cols - 1 + (rows - 1) * cols // 2, row_send, row_recv),
        (col_panel, pairs - 1, col_send, col_recv),
        (row_panel, (rows - 1) * cols // 2, across_send, None),
    ):
        part_of = panel.at[pl.ds(0, count)]
        if received is not None:
            pltpu.make_async_copy(part_of, part_of, received).wait()
        pltpu.make_async_copy(part_of, part_of, sent).wait()


def balanced(rows, cols):
    phases, per_row = cols // 2, cols // rows
    last = []
    for row in range(rows):
        own = (phases - 1 + (phases // 2 if row < rows // 2 else 0)) % phases
        last.append([own // per_row, (own + phases) // per_row])
    return all(
        sum(row in last[other] for other in range(rows) if other != row)
        == sum(target != row for target in last[row])
        for row in range(rows)
    )


def transform(product, pw_index, row_count, col_count, *bands):
    bands = [values.reshape(1, -1) for values in bands]
    points = product.shape[0]
    count = pw_index.shape[0]
    pairs = row_count * col_count
    lines = 2 * count // LANES
    tall, short = lines // row_count, lines // col_count
    tables = [jnp.asarray(table) for table in fourier_tables(points)]
    depth = 1024
    dma = pltpu.SemaphoreType.DMA
    operands = [product, pw_index.reshape(1, count), *tables, *bands]
    operands = [pltpu.with_memory_space_constraint(value, pltpu.HBM) for value in operands]
    return pl.pallas_call(
        functools.partial(transform_kernel, balanced(row_count, col_count)),
        out_shape=(
            pltpu.VMEM((pairs, tall // short, short, LANES), jnp.bfloat16),
            pltpu.VMEM((pairs, short, LANES), jnp.bfloat16),
            pltpu.VMEM((bands[0].shape[1], bands[-1].shape[1]), jnp.float32),
        ),
        in_specs=[pl.BlockSpec(memory_space=pltpu.HBM)] * len(operands),
        out_specs=(pl.BlockSpec(memory_space=pltpu.VMEM),) * 3,
        scratch_shapes=[pltpu.VMEM(value.shape, value.dtype) for value in operands] + [
            pltpu.VMEM((points * points, 2 * points), jnp.float32),
            pltpu.VMEM((points**3 // depth, depth), jnp.bfloat16),
            pltpu.VMEM((2 * short, LANES), jnp.float32),
            pltpu.VMEM((col_count, short, LANES), jnp.bfloat16),
            dma((len(operands) - 1,)), dma((points // min(16, points),)),
            dma, dma, dma, dma, dma, dma((row_count, col_count // 2, tall // short)),
        ],
        compiler_params=pltpu.CompilerParams(collective_id=0, has_side_effects=True),
        name="spectrum",
    )(*operands)


def product_kernel(row_ref, col_ref, weight_ref, out_ref, row_lines, col_lines, left, right, ring, sems):
    pairs = row_ref.shape[0]
    freq_count, row_width, _ = out_ref.shape
    slots, height = ring.shape[0], ring.shape[1]

    for ref, lines, is_left in ((row_ref, row_lines, True), (col_ref, col_lines, False)):
        if len(ref.shape) == 3:
            blocks = ref.shape[1]
            lines[...] = ref[...].astype(jnp.float32).reshape(lines.shape)
        else:
            blocks = ref.shape[1] // LANES
        for block in range(0 if is_left else blocks):
            lanes = slice(block * LANES, (block + 1) * LANES)
            if len(ref.shape) == 3:
                values = lines[pl.ds(block, pairs, stride=blocks), :]
            else:
                values = ref[:, lanes].astype(jnp.float32)
            if not is_left:
                for freq in range(freq_count):
                    right[freq, :, lanes] = (
                        values * weight_ref[:, freq:freq + 1]
                    ).astype(jnp.bfloat16)

    steps = row_width // height

    def write(slot, freq, step):
        rows = pl.ds(pl.multiple_of(step * height, height), height)
        return pltpu.make_async_copy(ring.at[slot], out_ref.at[freq, rows], sems.at[slot])

    @pl.loop(0, steps)
    def _(step):
        for part in range(height // LANES):
            block = step * (height // LANES) + part
            if len(row_ref.shape) == 3:
                values = row_lines[pl.ds(block, pairs, stride=row_ref.shape[1]), :]
            else:
                values = row_ref[:, pl.ds(pl.multiple_of(block * LANES, LANES), LANES)]
                values = values.astype(jnp.float32)
            left[part * LANES:(part + 1) * LANES, :] = values.T.astype(jnp.bfloat16)
        panel = left[...]
        for freq in range(freq_count):
            unit = step * freq_count + freq
            slot = lax.rem(unit, slots)

            @pl.when(unit >= slots)
            def _():
                write(slot, freq, step).wait()

            ring[slot] = dot(panel, right[freq])
            write(slot, freq, step).start()

    for slot in range(min(slots, steps * freq_count)):
        write(slot, 0, 0).wait()


def product(row_panel, col_panel, weights):
    pairs, freq_count = weights.shape
    row_panel = row_panel.reshape(pairs, -1, LANES)
    row_width = row_panel.shape[1] * LANES
    col_width = col_panel.shape[1] * LANES
    panels = []
    lines = []
    for panel in (row_panel, col_panel):
        height = panel.shape[1]
        if height % 16 == 0:
            panels.append(pltpu.with_memory_space_constraint(panel, pltpu.VMEM))
            lines.append(pltpu.VMEM((pairs * height, LANES), jnp.float32))
        else:
            panels.append(panel.reshape(pairs, height * LANES))
            lines.append(pltpu.VMEM((8, LANES), jnp.float32))
    block = min(256, row_width)
    slots = 4
    whole = pl.BlockSpec(memory_space=pltpu.VMEM)
    return pl.pallas_call(
        product_kernel,
        out_shape=jax.ShapeDtypeStruct((freq_count, row_width, col_width), jnp.float32),
        in_specs=[whole, whole, whole],
        out_specs=pl.BlockSpec(memory_space=pl.ANY),
        scratch_shapes=lines + [
            pltpu.VMEM((block, pairs), jnp.bfloat16),
            pltpu.VMEM((freq_count, pairs, col_width), jnp.bfloat16),
            pltpu.VMEM((slots, block, col_width), jnp.float32),
            pltpu.SemaphoreType.DMA((slots,)),
        ],
        name="product",
    )(*panels, pltpu.with_memory_space_constraint(weights, pltpu.VMEM))


def shards(
    pair_products,
    pw_index,
    valence_band,
    conduction_band,
    valence_energy,
    conduction_energy,
    imag_freq,
):
    rows, cols = lax.axis_size("row"), lax.axis_size("col")
    row_panel, col_panel, weights = transform(
        pair_products[0], pw_index, rows, cols,
        valence_band, conduction_band, valence_energy, conduction_energy, imag_freq,
    )
    return product(row_panel, col_panel, weights)


def solution(mesh):
    in_specs = (P(("row", "col"), None, None, None), P(), P(), P(), P(), P(), P())
    out_specs = P(None, "row", "col")
    return jax.shard_map(shards, mesh=mesh, in_specs=in_specs, out_specs=out_specs, check_vma=False)
```

```python
import functools
import math

import jax
import jax.numpy as jnp
import numpy as np
from jax import lax
from jax.experimental import pallas as pl
from jax.experimental.pallas import tpu as pltpu
from jax.sharding import PartitionSpec as P

MESH = pl.DeviceIdType.MESH
LANES = 128


def split(values):
    high = values.astype(jnp.bfloat16)
    low = (values - high.astype(jnp.float32)).astype(jnp.bfloat16)
    return high, low


def fourier_tables(points):
    counter = np.arange(points)
    angles = (counter[:, None] * counter[None, :] % points) * (2.0 * math.pi / points)
    cosine, sine = np.cos(angles), np.sin(angles)
    upper = points // 2

    def halves(table):
        single = table.astype(np.float32)
        high = single.astype(jnp.bfloat16)
        return high, (single - high.astype(np.float32)).astype(jnp.bfloat16)

    along_z = np.concatenate(halves(np.concatenate([cosine, -sine], axis=1)), axis=0)
    high, low = halves(np.concatenate([cosine, sine], axis=0))
    along_y = np.concatenate([high, high, low], axis=1)
    scale = float(points) ** (-1.5)
    high, low = halves(np.concatenate([cosine[:upper], sine[:upper]], axis=0) * scale)
    along_x = np.concatenate([high, high, low], axis=1)
    return [along_z, along_y, along_x]


def dot(left, right):
    return lax.dot_general(
        left, right, (((1,), (0,)), ((), ())), preferred_element_type=jnp.float32
    )


def column_of(row):
    size = row.shape[1]
    here = lax.broadcasted_iota(jnp.int32, (size, size), 0)
    there = lax.broadcasted_iota(jnp.int32, (size, size), 1)
    return jnp.sum(jnp.where(here == there, row, 0.0), axis=1, keepdims=True)


def lookup(indices, table):
    column = column_of(indices.astype(jnp.float32))
    slots = lax.broadcasted_iota(jnp.int32, (column.shape[0], table.shape[1]), 1)
    return jnp.sum(
        jnp.where(column == slots.astype(jnp.float32), table, 0.0), axis=1, keepdims=True
    )


def transform_kernel(
    direct_last, x_hbm, index_hbm, z_hbm, y_hbm, x_table_hbm,
    valence_band_hbm, conduction_band_hbm, valence_energy_hbm, conduction_energy_hbm, imag_freq_hbm,
    row_panel, col_panel, weights,
    x_ref, index_ref, z_ref, y_ref, x_table_ref,
    valence_band, conduction_band, valence_energy, conduction_energy, imag_freq,
    planes, spectrum, picked, staged,
    loaded, chunk_loaded, row_send, row_recv, col_send, col_recv, across_send, across_recv,
):
    cols, short = staged.shape[:2]
    per_row = row_panel.shape[1]
    rows = cols // per_row
    pairs = rows * cols
    phases = cols // 2
    r, c = lax.axis_index("row"), lax.axis_index("col")

    points = x_ref.shape[0]
    upper = points // 2
    wide = 2 * points
    step = min(32, points)
    chunks = points // step

    def chunk(at):
        planes_of = pl.ds(at * step, step)
        return pltpu.make_async_copy(x_hbm.at[planes_of], x_ref.at[planes_of], chunk_loaded.at[at])

    operands = [
        (z_hbm, z_ref), (y_hbm, y_ref), (x_table_hbm, x_table_ref), (index_hbm, index_ref),
        (valence_band_hbm, valence_band), (conduction_band_hbm, conduction_band),
        (valence_energy_hbm, valence_energy), (conduction_energy_hbm, conduction_energy),
        (imag_freq_hbm, imag_freq),
    ]

    def load(at):
        source, target = operands[at]
        return pltpu.make_async_copy(source, target, loaded.at[at])

    load(0).start()
    chunk(0).start()
    load(1).start()
    for at in range(1, chunks):
        chunk(at).start()
    for at in range(2, len(operands)):
        load(at).start()

    def ahead(i):
        return lax.rem(r + i, rows)

    def onward(k):
        return lax.rem(c + k, cols)

    def loop(first, last, action):
        def body(at, carry):
            action(at)
            return carry

        lax.fori_loop(first, last, body, 0, unroll=last - first <= 8)

    barrier = pltpu.get_barrier_semaphore()

    def greet(at):
        pl.semaphore_signal(
            barrier, inc=1, device_id=(ahead(at // cols), onward(lax.rem(at, cols))),
            device_id_type=MESH)

    loop(1, pairs, greet)

    load(0).wait()
    load(1).wait()
    along_z, along_y = z_ref[...], y_ref[...]
    sign = jnp.where(lax.broadcasted_iota(jnp.int32, (points, wide), 1) < points, 1.0, -1.0)

    for at in range(chunks):
        chunk(at).wait()
    for at in range(chunks):
        start = at * step
        data = x_ref[start:start + step].reshape(step * points, points)
        lines = dot(jnp.concatenate([data, data], axis=1), along_z)
        high, low = split(lines)
        for pair in range(step // 2):
            blocks = []
            for side in range(2):
                lot = slice((2 * pair + side) * points, (2 * pair + side + 1) * points)
                blocks.append(jnp.concatenate([high[lot], low[lot], high[lot]], axis=0))
            result = dot(along_y, jnp.concatenate(blocks, axis=1))
            for side in range(2):
                part = result[:, side * wide:(side + 1) * wide]
                first = (start + 2 * pair + side) * points
                planes[first:first + points, :] = (
                    part[:points] + sign * pltpu.roll(part[points:], points, 1)
                )

    load(2).wait()
    along_x = x_table_ref[...]
    per_group = spectrum.shape[1] // LANES
    groups = points // 2 // per_group
    half_rows = groups * upper
    first_half = lax.broadcasted_iota(jnp.int32, (upper, wide), 1) < points

    for group in range(groups):

        @pl.loop(0, per_group, unroll=8)
        def _(place):
            base = 2 * (group * per_group + place)
            blocks = []
            for side in range(2):
                high, low = split(planes[pl.ds(base + side, points, stride=points), :])
                blocks.append(jnp.concatenate([high, low, high], axis=0))
            result = dot(along_x, jnp.concatenate(blocks, axis=1))
            even_cos, odd_cos = result[:upper, :wide], result[:upper, wide:]
            even_sin, odd_sin = result[upper:, :wide], result[upper:, wide:]

            def join(left, right, turn_left, turn_right):
                left = pltpu.roll(left, points, 1) if turn_left else left
                right = pltpu.roll(right, points, 1) if turn_right else right
                return jnp.where(first_half, left, right)

            real = join(even_cos, odd_cos, False, True) + join(even_sin, odd_sin, True, False)
            imag = join(even_sin, odd_sin, False, True) - join(even_cos, odd_cos, True, False)
            columns = pl.ds(pl.multiple_of(place * LANES, LANES), LANES)
            spectrum[group * upper:(group + 1) * upper, columns] = real.astype(jnp.bfloat16)
            spectrum[half_rows + group * upper:half_rows + (group + 1) * upper, columns] = (
                imag.astype(jnp.bfloat16)
            )

    depth = spectrum.shape[1]
    width = 256
    part = 256
    local = lax.broadcasted_iota(jnp.int32, (part, width), 0).astype(jnp.float32).astype(jnp.bfloat16)
    row_of = lax.broadcasted_iota(jnp.int32, (half_rows, width), 0)
    one = jnp.ones((part, width), jnp.bfloat16)
    zero = jnp.zeros((part, width), jnp.bfloat16)

    lines_per_step = width // LANES
    steps = short // lines_per_step
    load(3).wait()

    def select(own, step):
        line = step * lines_per_step
        start = pl.multiple_of((own * short + line) * LANES, width)
        index = index_ref[:, pl.ds(start, width)]
        column = index % depth
        upper_part = index // depth
        row = (upper_part % groups) * upper + upper_part // groups
        total = jnp.zeros((2 * half_rows, width), jnp.float32)
        for at in range(depth // part):
            shifted = (column - at * part).astype(jnp.float32).astype(jnp.bfloat16)
            chosen = jnp.where(local == jnp.broadcast_to(shifted, local.shape), one, zero)
            total = total + dot(spectrum[:, at * part:(at + 1) * part], chosen)
        mask = row_of == row
        real = jnp.sum(jnp.where(mask, total[:half_rows], 0.0), axis=0, keepdims=True)
        imag = jnp.sum(jnp.where(mask, total[half_rows:], 0.0), axis=0, keepdims=True)
        for side in range(lines_per_step):
            lanes = slice(side * LANES, (side + 1) * LANES)
            picked[pl.ds(line + side, 1), :] = real[:, lanes]
            picked[pl.ds(short + line + side, 1), :] = imag[:, lanes]

    def row_copy(own, k):
        return pltpu.make_async_remote_copy(
            src_ref=staged.at[own], dst_ref=row_panel.at[r * cols + c, lax.rem(own, per_row)],
            send_sem=row_send, recv_sem=row_recv,
            device_id=(own // per_row, onward(k)), device_id_type=MESH)

    parity = lax.rem(c, 2)

    def across(own, at):
        lot = lax.rem(own, per_row)
        return pltpu.make_async_remote_copy(
            src_ref=staged.at[own], dst_ref=row_panel.at[r * cols + c, lot],
            send_sem=across_send, recv_sem=across_recv.at[r, c // 2, lot],
            device_id=(own // per_row, 2 * at + parity), device_id_type=MESH)

    def other_core(own, at):
        return pltpu.make_async_remote_copy(
            src_ref=staged.at[own], dst_ref=row_panel.at[r * cols + c, lax.rem(own, per_row)],
            send_sem=row_send, recv_sem=row_recv,
            device_id=(own // per_row, 2 * at + 1 - parity), device_id_type=MESH)

    def pass_on(held):
        return pltpu.make_async_remote_copy(
            src_ref=held, dst_ref=held, send_sem=row_send, recv_sem=row_recv,
            device_id=(r, c + 1 - 2 * parity), device_id_type=MESH)

    def col_copy(own, i):
        return pltpu.make_async_remote_copy(
            src_ref=staged.at[own], dst_ref=col_panel.at[r * cols + c],
            send_sem=col_send, recv_sem=col_recv,
            device_id=(ahead(i), own), device_id_type=MESH)

    def is_direct(phase):
        return direct_last and phase == phases - 1

    def distribute(own, phase):
        inside = own // per_row == r

        @pl.when(jnp.logical_not(inside))
        def _():
            loop(0, cols // 2, lambda at: across(own, at).start())
            if is_direct(phase):
                loop(0, cols // 2, lambda at: other_core(own, at).start())

        @pl.when(inside)
        def _():
            loop(1, cols, lambda k: row_copy(own, k).start())

        loop(1, rows, lambda i: col_copy(own, i).start())

        @pl.when(own != c)
        def _():
            col_copy(own, 0).start()

        @pl.when(inside)
        def _():
            row_panel[r * cols + c, lax.rem(own, per_row)] = staged[own]

        @pl.when(own == c)
        def _():
            col_panel[r * cols + c] = staged[own]

    def turn_of(row):
        return jnp.where(row < rows // 2, phases // 2, 0)

    def relay(phase, which):
        def one(i):
            source = ahead(i)
            own = lax.rem(phase + turn_of(source), phases)
            for side in range(2):
                group = own + side * phases
                mine = group // per_row == r
                if which == "early":
                    mine = jnp.logical_and(mine, source < r)
                elif which == "late":
                    mine = jnp.logical_and(mine, source > r)

                @pl.when(mine)
                def _():
                    lot = lax.rem(group, per_row)

                    def take(at):
                        held = row_panel.at[source * cols + 2 * at + parity, lot]
                        pltpu.make_async_copy(held, held, across_recv.at[source, at, lot]).wait()
                        if not is_direct(phase):
                            pass_on(held).start()

                    loop(0, cols // 2, take)

        loop(1, rows, one)

    for phase in range(phases):
        own = lax.rem(phase + turn_of(r), phases)

        @pl.loop(0, steps, unroll=min(8, steps))
        def _(step):
            select(own, step)

        for side in range(2):
            staged[own + side * phases] = picked[side * short:(side + 1) * short, :].astype(jnp.bfloat16)
        if phase == 0:
            pl.semaphore_wait(barrier, pairs - 1)
        for side in range(2):
            distribute(own + side * phases, phase)
        if phase >= 2:
            relay(phase - 2, "early")

    for at in range(4, len(operands)):
        load(at).wait()
    gap = lookup(conduction_band[...], conduction_energy[...]) - lookup(
        valence_band[...], valence_energy[...]
    )
    root = math.sqrt(gap.shape[0])
    for freq in range(weights.shape[1]):
        omega = imag_freq[:, freq:freq + 1]
        weights[:, freq:freq + 1] = -4.0 * gap / (gap * gap + omega * omega) / root

    for phase in range(phases):
        relay(phase, "late" if phase < phases - 2 else "all")

    for panel, count, sent, received in (
        (row_panel, cols - 1 + (rows - 1) * cols // 2, row_send, row_recv),
        (col_panel, pairs - 1, col_send, col_recv),
        (row_panel, (rows - 1) * cols // 2, across_send, None),
    ):
        part_of = panel.at[pl.ds(0, count)]
        if received is not None:
            pltpu.make_async_copy(part_of, part_of, received).wait()
        pltpu.make_async_copy(part_of, part_of, sent).wait()


def balanced(rows, cols):
    phases, per_row = cols // 2, cols // rows
    last = []
    for row in range(rows):
        own = (phases - 1 + (phases // 2 if row < rows // 2 else 0)) % phases
        last.append([own // per_row, (own + phases) // per_row])
    return all(
        sum(row in last[other] for other in range(rows) if other != row)
        == sum(target != row for target in last[row])
        for row in range(rows)
    )


def transform(product, pw_index, row_count, col_count, *bands):
    bands = [values.reshape(1, -1) for values in bands]
    points = product.shape[0]
    count = pw_index.shape[0]
    pairs = row_count * col_count
    lines = 2 * count // LANES
    tall, short = lines // row_count, lines // col_count
    tables = [jnp.asarray(table) for table in fourier_tables(points)]
    depth = 1024
    dma = pltpu.SemaphoreType.DMA
    operands = [product, pw_index.reshape(1, count), *tables, *bands]
    operands = [pltpu.with_memory_space_constraint(value, pltpu.HBM) for value in operands]
    return pl.pallas_call(
        functools.partial(transform_kernel, balanced(row_count, col_count)),
        out_shape=(
            pltpu.VMEM((pairs, tall // short, short, LANES), jnp.bfloat16),
            pltpu.VMEM((pairs, short, LANES), jnp.bfloat16),
            pltpu.VMEM((bands[0].shape[1], bands[-1].shape[1]), jnp.float32),
        ),
        in_specs=[pl.BlockSpec(memory_space=pltpu.HBM)] * len(operands),
        out_specs=(pl.BlockSpec(memory_space=pltpu.VMEM),) * 3,
        scratch_shapes=[pltpu.VMEM(value.shape, value.dtype) for value in operands] + [
            pltpu.VMEM((points * points, 2 * points), jnp.float32),
            pltpu.VMEM((points**3 // depth, depth), jnp.bfloat16),
            pltpu.VMEM((2 * short, LANES), jnp.float32),
            pltpu.VMEM((col_count, short, LANES), jnp.bfloat16),
            dma((len(operands) - 1,)), dma((points // min(32, points),)),
            dma, dma, dma, dma, dma, dma((row_count, col_count // 2, tall // short)),
        ],
        compiler_params=pltpu.CompilerParams(collective_id=0, has_side_effects=True),
        name="spectrum",
    )(*operands)


def product_kernel(row_ref, col_ref, weight_ref, out_ref, row_lines, col_lines, left, right, ring, sems):
    pairs = row_ref.shape[0]
    freq_count, row_width, _ = out_ref.shape
    slots, height = ring.shape[0], ring.shape[1]
    wide = [
        jnp.broadcast_to(weight_ref[:, freq:freq + 1], (pairs, LANES)) for freq in range(freq_count)
    ]
    stacked = len(col_ref.shape) == 3
    col_blocks = col_ref.shape[1] if stacked else col_ref.shape[1] // LANES
    if stacked:
        col_lines[...] = col_ref[...].astype(jnp.float32).reshape(col_lines.shape)
    if len(row_ref.shape) == 3:
        row_lines[...] = row_ref[...].astype(jnp.float32).reshape(row_lines.shape)

    def weigh(freq):
        for block in range(col_blocks):
            lanes = slice(block * LANES, (block + 1) * LANES)
            if stacked:
                values = col_lines[pl.ds(block, pairs, stride=col_blocks), :]
            else:
                values = col_ref[:, lanes].astype(jnp.float32)
            right[freq, :, lanes] = (values * wide[freq]).astype(jnp.bfloat16)

    def turn(step, part):
        block = step * (height // LANES) + part
        if len(row_ref.shape) == 3:
            values = row_lines[pl.ds(block, pairs, stride=row_ref.shape[1]), :]
        else:
            values = row_ref[:, pl.ds(pl.multiple_of(block * LANES, LANES), LANES)]
            values = values.astype(jnp.float32)
        left[part * LANES:(part + 1) * LANES, :] = values.T.astype(jnp.bfloat16)

    steps = row_width // height

    def write(slot, freq, step):
        rows = pl.ds(pl.multiple_of(step * height, height), height)
        return pltpu.make_async_copy(ring.at[slot], out_ref.at[freq, rows], sems.at[slot])

    lead = LANES // 2
    for freq in range(freq_count):
        weigh(freq)
        for first in range(0, height, lead):
            if freq == 0 and first % LANES == 0:
                turn(0, first // LANES)
            rows = slice(first, first + lead)
            ring[freq, rows] = dot(left[rows], right[freq])
            pltpu.make_async_copy(
                ring.at[freq, rows], out_ref.at[freq, rows], sems.at[freq]
            ).start()

    @pl.loop(1, steps)
    def _(step):
        for part in range(height // LANES):
            turn(step, part)
        panel = left[...]
        for freq in range(freq_count):
            unit = step * freq_count + freq
            slot = lax.rem(unit, slots)

            @pl.when(unit >= slots)
            def _():
                write(slot, freq, step).wait()

            ring[slot] = dot(panel, right[freq])
            write(slot, freq, step).start()

    for slot in range(min(slots, steps * freq_count)):
        write(slot, 0, 0).wait()


def product(row_panel, col_panel, weights):
    pairs, freq_count = weights.shape
    row_panel = row_panel.reshape(pairs, -1, LANES)
    row_width = row_panel.shape[1] * LANES
    col_width = col_panel.shape[1] * LANES
    panels = []
    lines = []
    for panel in (row_panel, col_panel):
        height = panel.shape[1]
        if height % 16 == 0:
            panels.append(pltpu.with_memory_space_constraint(panel, pltpu.VMEM))
            lines.append(pltpu.VMEM((pairs * height, LANES), jnp.float32))
        else:
            panels.append(panel.reshape(pairs, height * LANES))
            lines.append(pltpu.VMEM((8, LANES), jnp.float32))
    block = min(256, row_width)
    slots = max(4, freq_count)
    whole = pl.BlockSpec(memory_space=pltpu.VMEM)
    return pl.pallas_call(
        product_kernel,
        out_shape=jax.ShapeDtypeStruct((freq_count, row_width, col_width), jnp.float32),
        in_specs=[whole, whole, whole],
        out_specs=pl.BlockSpec(memory_space=pl.ANY),
        scratch_shapes=lines + [
            pltpu.VMEM((block, pairs), jnp.bfloat16),
            pltpu.VMEM((freq_count, pairs, col_width), jnp.bfloat16),
            pltpu.VMEM((slots, block, col_width), jnp.float32),
            pltpu.SemaphoreType.DMA((slots,)),
        ],
        name="product",
    )(*panels, pltpu.with_memory_space_constraint(weights, pltpu.VMEM))


def shards(
    pair_products,
    pw_index,
    valence_band,
    conduction_band,
    valence_energy,
    conduction_energy,
    imag_freq,
):
    rows, cols = lax.axis_size("row"), lax.axis_size("col")
    row_panel, col_panel, weights = transform(
        pair_products[0], pw_index, rows, cols,
        valence_band, conduction_band, valence_energy, conduction_energy, imag_freq,
    )
    return product(row_panel, col_panel, weights)


def solution(mesh):
    in_specs = (P(("row", "col"), None, None, None), P(), P(), P(), P(), P(), P())
    out_specs = P(None, "row", "col")
    return jax.shard_map(shards, mesh=mesh, in_specs=in_specs, out_specs=out_specs, check_vma=False)
```

```python
import functools
import math

import jax
import jax.numpy as jnp
import numpy as np
from jax import lax
from jax.experimental import pallas as pl
from jax.experimental.pallas import tpu as pltpu
from jax.sharding import PartitionSpec as P

MESH = pl.DeviceIdType.MESH
LANES = 128


def split(values):
    high = values.astype(jnp.bfloat16)
    low = (values - high.astype(jnp.float32)).astype(jnp.bfloat16)
    return high, low


def fourier_tables(points):
    counter = np.arange(points)
    angles = (counter[:, None] * counter[None, :] % points) * (2.0 * math.pi / points)
    cosine, sine = np.cos(angles), np.sin(angles)
    upper = points // 2

    def halves(table):
        single = table.astype(np.float32)
        high = single.astype(jnp.bfloat16)
        return high, (single - high.astype(np.float32)).astype(jnp.bfloat16)

    along_z = np.concatenate(halves(np.concatenate([cosine, -sine], axis=1)), axis=0)
    high, low = halves(np.concatenate([cosine, sine], axis=0))
    along_y = np.concatenate([high, high, low], axis=1)
    scale = float(points) ** (-1.5)
    high, low = halves(np.concatenate([cosine[:upper], sine[:upper]], axis=0) * scale)
    along_x = np.concatenate([high, high, low], axis=1)
    return [along_z, along_y, along_x]


def dot(left, right):
    return lax.dot_general(
        left, right, (((1,), (0,)), ((), ())), preferred_element_type=jnp.float32
    )


def column_of(row):
    size = row.shape[1]
    here = lax.broadcasted_iota(jnp.int32, (size, size), 0)
    there = lax.broadcasted_iota(jnp.int32, (size, size), 1)
    return jnp.sum(jnp.where(here == there, row, 0.0), axis=1, keepdims=True)


def lookup(indices, table):
    column = column_of(indices.astype(jnp.float32))
    slots = lax.broadcasted_iota(jnp.int32, (column.shape[0], table.shape[1]), 1)
    return jnp.sum(
        jnp.where(column == slots.astype(jnp.float32), table, 0.0), axis=1, keepdims=True
    )


def transform_kernel(
    direct_last, x_hbm, index_hbm, z_hbm, y_hbm, x_table_hbm,
    valence_band_hbm, conduction_band_hbm, valence_energy_hbm, conduction_energy_hbm, imag_freq_hbm,
    row_panel, col_panel, weights,
    x_ref, index_ref, z_ref, y_ref, x_table_ref,
    valence_band, conduction_band, valence_energy, conduction_energy, imag_freq,
    planes, spectrum, picked, staged,
    loaded, chunk_loaded, row_send, row_recv, col_send, col_recv, across_send, across_recv,
):
    cols, short = staged.shape[:2]
    per_row = row_panel.shape[1]
    rows = cols // per_row
    pairs = rows * cols
    phases = cols // 2
    r, c = lax.axis_index("row"), lax.axis_index("col")

    points = x_ref.shape[0]
    upper = points // 2
    wide = 2 * points
    step = min(32, points)
    chunks = points // step

    def chunk(at):
        planes_of = pl.ds(at * step, step)
        return pltpu.make_async_copy(x_hbm.at[planes_of], x_ref.at[planes_of], chunk_loaded.at[at])

    operands = [
        (z_hbm, z_ref), (y_hbm, y_ref), (x_table_hbm, x_table_ref), (index_hbm, index_ref),
        (valence_band_hbm, valence_band), (conduction_band_hbm, conduction_band),
        (valence_energy_hbm, valence_energy), (conduction_energy_hbm, conduction_energy),
        (imag_freq_hbm, imag_freq),
    ]

    def load(at):
        source, target = operands[at]
        return pltpu.make_async_copy(source, target, loaded.at[at])

    load(0).start()
    chunk(0).start()
    load(1).start()
    for at in range(1, chunks):
        chunk(at).start()
    for at in range(2, len(operands)):
        load(at).start()

    def ahead(i):
        return lax.rem(r + i, rows)

    def onward(k):
        return lax.rem(c + k, cols)

    def loop(first, last, action):
        def body(at, carry):
            action(at)
            return carry

        lax.fori_loop(first, last, body, 0, unroll=last - first <= 8)

    barrier = pltpu.get_barrier_semaphore()

    def greet(at):
        pl.semaphore_signal(
            barrier, inc=1, device_id=(ahead(at // cols), onward(lax.rem(at, cols))),
            device_id_type=MESH)

    loop(1, pairs, greet)

    load(0).wait()
    load(1).wait()
    along_z, along_y = z_ref[...], y_ref[...]
    sign = jnp.where(lax.broadcasted_iota(jnp.int32, (points, wide), 1) < points, 1.0, -1.0)

    for at in range(chunks):
        chunk(at).wait()
    for at in range(chunks):
        start = at * step
        data = x_ref[start:start + step].reshape(step * points, points)
        lines = dot(jnp.concatenate([data, data], axis=1), along_z)
        high, low = split(lines)
        for pair in range(step // 2):
            blocks = []
            for side in range(2):
                lot = slice((2 * pair + side) * points, (2 * pair + side + 1) * points)
                blocks.append(jnp.concatenate([high[lot], low[lot], high[lot]], axis=0))
            result = dot(along_y, jnp.concatenate(blocks, axis=1))
            for side in range(2):
                part = result[:, side * wide:(side + 1) * wide]
                first = (start + 2 * pair + side) * points
                planes[first:first + points, :] = (
                    part[:points] + sign * pltpu.roll(part[points:], points, 1)
                )

    load(2).wait()
    along_x = x_table_ref[...]
    per_group = spectrum.shape[1] // LANES
    groups = points // 2 // per_group
    half_rows = groups * upper
    first_half = lax.broadcasted_iota(jnp.int32, (upper, wide), 1) < points

    for group in range(groups):

        @pl.loop(0, per_group, unroll=8)
        def _(place):
            base = 2 * (group * per_group + place)
            blocks = []
            for side in range(2):
                high, low = split(planes[pl.ds(base + side, points, stride=points), :])
                blocks.append(jnp.concatenate([high, low, high], axis=0))
            result = dot(along_x, jnp.concatenate(blocks, axis=1))
            even_cos, odd_cos = result[:upper, :wide], result[:upper, wide:]
            even_sin, odd_sin = result[upper:, :wide], result[upper:, wide:]

            def join(left, right, turn_left, turn_right):
                left = pltpu.roll(left, points, 1) if turn_left else left
                right = pltpu.roll(right, points, 1) if turn_right else right
                return jnp.where(first_half, left, right)

            real = join(even_cos, odd_cos, False, True) + join(even_sin, odd_sin, True, False)
            imag = join(even_sin, odd_sin, False, True) - join(even_cos, odd_cos, True, False)
            columns = pl.ds(pl.multiple_of(place * LANES, LANES), LANES)
            spectrum[group * upper:(group + 1) * upper, columns] = real.astype(jnp.bfloat16)
            spectrum[half_rows + group * upper:half_rows + (group + 1) * upper, columns] = (
                imag.astype(jnp.bfloat16)
            )

    depth = spectrum.shape[1]
    width = 256
    part = 256
    local = lax.broadcasted_iota(jnp.int32, (part, width), 0).astype(jnp.float32).astype(jnp.bfloat16)
    row_of = lax.broadcasted_iota(jnp.int32, (upper, width), 0)
    one = jnp.ones((part, width), jnp.bfloat16)
    zero = jnp.zeros((part, width), jnp.bfloat16)

    lines_per_step = width // LANES
    steps = short // lines_per_step
    load(3).wait()

    def select(own, step):
        line = step * lines_per_step
        start = pl.multiple_of((own * short + line) * LANES, width)
        index = index_ref[:, pl.ds(start, width)]
        column = index & (depth - 1)
        upper_part = index >> (depth.bit_length() - 1)
        block_of = column // part
        inside = (column % part).astype(jnp.float32).astype(jnp.bfloat16)
        hit = jnp.where(local == jnp.broadcast_to(inside, local.shape), one, zero)
        total = jnp.zeros((2 * half_rows, width), jnp.float32)
        for at in range(depth // part):
            flag = jnp.where(block_of == at, 1.0, 0.0).astype(jnp.bfloat16)
            total = total + dot(spectrum[:, at * part:(at + 1) * part], hit * flag)
        among = upper_part % groups
        mask = row_of == upper_part // groups

        def pick(half):
            kept = half[:upper]
            for group in range(1, groups):
                kept = jnp.where(among == group, half[group * upper:(group + 1) * upper], kept)
            return jnp.sum(jnp.where(mask, kept, 0.0), axis=0, keepdims=True)

        real, imag = pick(total[:half_rows]), pick(total[half_rows:])
        for side in range(lines_per_step):
            lanes = slice(side * LANES, (side + 1) * LANES)
            picked[pl.ds(line + side, 1), :] = real[:, lanes]
            picked[pl.ds(short + line + side, 1), :] = imag[:, lanes]

    def row_copy(own, k):
        return pltpu.make_async_remote_copy(
            src_ref=staged.at[own], dst_ref=row_panel.at[r * cols + c, lax.rem(own, per_row)],
            send_sem=row_send, recv_sem=row_recv,
            device_id=(own // per_row, onward(k)), device_id_type=MESH)

    parity = lax.rem(c, 2)

    def across(own, at):
        lot = lax.rem(own, per_row)
        return pltpu.make_async_remote_copy(
            src_ref=staged.at[own], dst_ref=row_panel.at[r * cols + c, lot],
            send_sem=across_send, recv_sem=across_recv.at[r, c // 2, lot],
            device_id=(own // per_row, 2 * at + parity), device_id_type=MESH)

    def other_core(own, at):
        return pltpu.make_async_remote_copy(
            src_ref=staged.at[own], dst_ref=row_panel.at[r * cols + c, lax.rem(own, per_row)],
            send_sem=row_send, recv_sem=row_recv,
            device_id=(own // per_row, 2 * at + 1 - parity), device_id_type=MESH)

    def pass_on(held):
        return pltpu.make_async_remote_copy(
            src_ref=held, dst_ref=held, send_sem=row_send, recv_sem=row_recv,
            device_id=(r, c + 1 - 2 * parity), device_id_type=MESH)

    def col_copy(own, i):
        return pltpu.make_async_remote_copy(
            src_ref=staged.at[own], dst_ref=col_panel.at[r * cols + c],
            send_sem=col_send, recv_sem=col_recv,
            device_id=(ahead(i), own), device_id_type=MESH)

    def is_direct(phase):
        return direct_last and phase == phases - 1

    def distribute(own, phase):
        inside = own // per_row == r

        @pl.when(jnp.logical_not(inside))
        def _():
            loop(0, cols // 2, lambda at: across(own, at).start())
            if is_direct(phase):
                loop(0, cols // 2, lambda at: other_core(own, at).start())

        @pl.when(inside)
        def _():
            loop(1, cols, lambda k: row_copy(own, k).start())

        loop(1, rows, lambda i: col_copy(own, i).start())

        @pl.when(own != c)
        def _():
            col_copy(own, 0).start()

        @pl.when(inside)
        def _():
            row_panel[r * cols + c, lax.rem(own, per_row)] = staged[own]

        @pl.when(own == c)
        def _():
            col_panel[r * cols + c] = staged[own]

    def turn_of(row):
        return jnp.where(row < rows // 2, phases // 2, 0)

    def relay(phase, which):
        def one(i):
            source = ahead(i)
            own = lax.rem(phase + turn_of(source), phases)
            for side in range(2):
                group = own + side * phases
                mine = group // per_row == r
                if which == "early":
                    mine = jnp.logical_and(mine, source < r)
                elif which == "late":
                    mine = jnp.logical_and(mine, source > r)

                @pl.when(mine)
                def _():
                    lot = lax.rem(group, per_row)

                    def take(at):
                        held = row_panel.at[source * cols + 2 * at + parity, lot]
                        pltpu.make_async_copy(held, held, across_recv.at[source, at, lot]).wait()
                        if not is_direct(phase):
                            pass_on(held).start()

                    loop(0, cols // 2, take)

        loop(1, rows, one)

    for phase in range(phases):
        own = lax.rem(phase + turn_of(r), phases)

        @pl.loop(0, steps, unroll=min(8, steps))
        def _(step):
            select(own, step)

        for side in range(2):
            staged[own + side * phases] = picked[side * short:(side + 1) * short, :].astype(jnp.bfloat16)
        if phase == 0:
            pl.semaphore_wait(barrier, pairs - 1)
        for side in range(2):
            distribute(own + side * phases, phase)
        if phase >= 2:
            relay(phase - 2, "early")

    for at in range(4, len(operands)):
        load(at).wait()
    gap = lookup(conduction_band[...], conduction_energy[...]) - lookup(
        valence_band[...], valence_energy[...]
    )
    root = math.sqrt(gap.shape[0])
    for freq in range(weights.shape[1]):
        omega = imag_freq[:, freq:freq + 1]
        weights[:, freq:freq + 1] = -4.0 * gap / (gap * gap + omega * omega) / root

    for phase in range(phases):
        relay(phase, "late" if phase < phases - 2 else "all")

    for panel, count, sent, received in (
        (row_panel, cols - 1 + (rows - 1) * cols // 2, row_send, row_recv),
        (col_panel, pairs - 1, col_send, col_recv),
        (row_panel, (rows - 1) * cols // 2, across_send, None),
    ):
        part_of = panel.at[pl.ds(0, count)]
        if received is not None:
            pltpu.make_async_copy(part_of, part_of, received).wait()
        pltpu.make_async_copy(part_of, part_of, sent).wait()


def balanced(rows, cols):
    phases, per_row = cols // 2, cols // rows
    last = []
    for row in range(rows):
        own = (phases - 1 + (phases // 2 if row < rows // 2 else 0)) % phases
        last.append([own // per_row, (own + phases) // per_row])
    return all(
        sum(row in last[other] for other in range(rows) if other != row)
        == sum(target != row for target in last[row])
        for row in range(rows)
    )


def transform(product, pw_index, row_count, col_count, *bands):
    bands = [values.reshape(1, -1) for values in bands]
    points = product.shape[0]
    count = pw_index.shape[0]
    pairs = row_count * col_count
    lines = 2 * count // LANES
    tall, short = lines // row_count, lines // col_count
    tables = [jnp.asarray(table) for table in fourier_tables(points)]
    depth = 1024
    dma = pltpu.SemaphoreType.DMA
    operands = [product, pw_index.reshape(1, count), *tables, *bands]
    operands = [pltpu.with_memory_space_constraint(value, pltpu.HBM) for value in operands]
    return pl.pallas_call(
        functools.partial(transform_kernel, balanced(row_count, col_count)),
        out_shape=(
            pltpu.VMEM((pairs, tall // short, short, LANES), jnp.bfloat16),
            pltpu.VMEM((pairs, short, LANES), jnp.bfloat16),
            pltpu.VMEM((bands[0].shape[1], bands[-1].shape[1]), jnp.float32),
        ),
        in_specs=[pl.BlockSpec(memory_space=pltpu.HBM)] * len(operands),
        out_specs=(pl.BlockSpec(memory_space=pltpu.VMEM),) * 3,
        scratch_shapes=[pltpu.VMEM(value.shape, value.dtype) for value in operands] + [
            pltpu.VMEM((points * points, 2 * points), jnp.float32),
            pltpu.VMEM((points**3 // depth, depth), jnp.bfloat16),
            pltpu.VMEM((2 * short, LANES), jnp.float32),
            pltpu.VMEM((col_count, short, LANES), jnp.bfloat16),
            dma((len(operands) - 1,)), dma((points // min(32, points),)),
            dma, dma, dma, dma, dma, dma((row_count, col_count // 2, tall // short)),
        ],
        compiler_params=pltpu.CompilerParams(collective_id=0, has_side_effects=True),
        name="spectrum",
    )(*operands)


def product_kernel(row_ref, col_ref, weight_ref, out_ref, row_lines, col_lines, left, right, ring, sems):
    pairs = row_ref.shape[0]
    freq_count, row_width, _ = out_ref.shape
    slots, height = ring.shape[0], ring.shape[1]
    wide = [
        jnp.broadcast_to(weight_ref[:, freq:freq + 1], (pairs, LANES)) for freq in range(freq_count)
    ]
    stacked = len(col_ref.shape) == 3
    col_blocks = col_ref.shape[1] if stacked else col_ref.shape[1] // LANES
    if stacked:
        col_lines[...] = col_ref[...].astype(jnp.float32).reshape(col_lines.shape)
    if len(row_ref.shape) == 3:
        row_lines[...] = row_ref[...].astype(jnp.float32).reshape(row_lines.shape)

    def weigh(freq):
        for block in range(col_blocks):
            lanes = slice(block * LANES, (block + 1) * LANES)
            if stacked:
                values = col_lines[pl.ds(block, pairs, stride=col_blocks), :]
            else:
                values = col_ref[:, lanes].astype(jnp.float32)
            right[freq, :, lanes] = (values * wide[freq]).astype(jnp.bfloat16)

    def turn(step, part):
        block = step * (height // LANES) + part
        if len(row_ref.shape) == 3:
            values = row_lines[pl.ds(block, pairs, stride=row_ref.shape[1]), :]
        else:
            values = row_ref[:, pl.ds(pl.multiple_of(block * LANES, LANES), LANES)]
            values = values.astype(jnp.float32)
        left[part * LANES:(part + 1) * LANES, :] = values.T.astype(jnp.bfloat16)

    steps = row_width // height

    def write(slot, freq, step):
        rows = pl.ds(pl.multiple_of(step * height, height), height)
        return pltpu.make_async_copy(ring.at[slot], out_ref.at[freq, rows], sems.at[slot])

    lead = LANES // 4
    for freq in range(freq_count):
        weigh(freq)
        for first in range(0, height, lead):
            if freq == 0 and first % LANES == 0:
                turn(0, first // LANES)
            rows = slice(first, first + lead)
            ring[freq, rows] = dot(left[rows], right[freq])
            pltpu.make_async_copy(
                ring.at[freq, rows], out_ref.at[freq, rows], sems.at[freq]
            ).start()

    @pl.loop(1, steps)
    def _(step):
        for part in range(height // LANES):
            turn(step, part)
        panel = left[...]
        for freq in range(freq_count):
            unit = step * freq_count + freq
            slot = lax.rem(unit, slots)

            @pl.when(unit >= slots)
            def _():
                write(slot, freq, step).wait()

            ring[slot] = dot(panel, right[freq])
            write(slot, freq, step).start()

    for slot in range(min(slots, steps * freq_count)):
        write(slot, 0, 0).wait()


def product(row_panel, col_panel, weights):
    pairs, freq_count = weights.shape
    row_panel = row_panel.reshape(pairs, -1, LANES)
    row_width = row_panel.shape[1] * LANES
    col_width = col_panel.shape[1] * LANES
    panels = []
    lines = []
    for panel in (row_panel, col_panel):
        height = panel.shape[1]
        if height % 16 == 0:
            panels.append(pltpu.with_memory_space_constraint(panel, pltpu.VMEM))
            lines.append(pltpu.VMEM((pairs * height, LANES), jnp.float32))
        else:
            panels.append(panel.reshape(pairs, height * LANES))
            lines.append(pltpu.VMEM((8, LANES), jnp.float32))
    block = min(256, row_width)
    slots = max(4, freq_count)
    whole = pl.BlockSpec(memory_space=pltpu.VMEM)
    return pl.pallas_call(
        product_kernel,
        out_shape=jax.ShapeDtypeStruct((freq_count, row_width, col_width), jnp.float32),
        in_specs=[whole, whole, whole],
        out_specs=pl.BlockSpec(memory_space=pl.ANY),
        scratch_shapes=lines + [
            pltpu.VMEM((block, pairs), jnp.bfloat16),
            pltpu.VMEM((freq_count, pairs, col_width), jnp.bfloat16),
            pltpu.VMEM((slots, block, col_width), jnp.float32),
            pltpu.SemaphoreType.DMA((slots,)),
        ],
        name="product",
    )(*panels, pltpu.with_memory_space_constraint(weights, pltpu.VMEM))


def shards(
    pair_products,
    pw_index,
    valence_band,
    conduction_band,
    valence_energy,
    conduction_energy,
    imag_freq,
):
    rows, cols = lax.axis_size("row"), lax.axis_size("col")
    row_panel, col_panel, weights = transform(
        pair_products[0], pw_index, rows, cols,
        valence_band, conduction_band, valence_energy, conduction_energy, imag_freq,
    )
    return product(row_panel, col_panel, weights)


def solution(mesh):
    in_specs = (P(("row", "col"), None, None, None), P(), P(), P(), P(), P(), P())
    out_specs = P(None, "row", "col")
    return jax.shard_map(shards, mesh=mesh, in_specs=in_specs, out_specs=out_specs, check_vma=False)
```

```python
import functools
import math

import jax
import jax.numpy as jnp
import numpy as np
from jax import lax
from jax.experimental import pallas as pl
from jax.experimental.pallas import tpu as pltpu
from jax.sharding import PartitionSpec as P

MESH = pl.DeviceIdType.MESH
LANES = 128


def split(values):
    high = values.astype(jnp.bfloat16)
    low = (values - high.astype(jnp.float32)).astype(jnp.bfloat16)
    return high, low


def fourier_tables(points):
    counter = np.arange(points)
    angles = (counter[:, None] * counter[None, :] % points) * (2.0 * math.pi / points)
    cosine, sine = np.cos(angles), np.sin(angles)
    upper = points // 2

    def halves(table):
        single = table.astype(np.float32)
        high = single.astype(jnp.bfloat16)
        return high, (single - high.astype(np.float32)).astype(jnp.bfloat16)

    along_z = np.concatenate(halves(np.concatenate([cosine, -sine], axis=1)), axis=0)
    high, low = halves(np.concatenate([cosine, sine], axis=0))
    along_y = np.concatenate([high, high, low], axis=1)
    scale = float(points) ** (-1.5)
    high, low = halves(np.concatenate([cosine[:upper], sine[:upper]], axis=0) * scale)
    along_x = np.concatenate([high, high, low], axis=1)
    return [along_z, along_y, along_x]


def dot(left, right):
    return lax.dot_general(
        left, right, (((1,), (0,)), ((), ())), preferred_element_type=jnp.float32
    )


def column_of(row):
    size = row.shape[1]
    here = lax.broadcasted_iota(jnp.int32, (size, size), 0)
    there = lax.broadcasted_iota(jnp.int32, (size, size), 1)
    return jnp.sum(jnp.where(here == there, row, 0.0), axis=1, keepdims=True)


def lookup(indices, table):
    column = column_of(indices.astype(jnp.float32))
    slots = lax.broadcasted_iota(jnp.int32, (column.shape[0], table.shape[1]), 1)
    return jnp.sum(
        jnp.where(column == slots.astype(jnp.float32), table, 0.0), axis=1, keepdims=True
    )


def transform_kernel(
    direct_last, x_hbm, index_hbm, z_hbm, y_hbm, x_table_hbm,
    valence_band_hbm, conduction_band_hbm, valence_energy_hbm, conduction_energy_hbm, imag_freq_hbm,
    row_panel, col_panel, weights,
    x_ref, index_ref, z_ref, y_ref, x_table_ref,
    valence_band, conduction_band, valence_energy, conduction_energy, imag_freq,
    planes, spectrum, picked, staged,
    loaded, chunk_loaded, row_send, row_recv, col_send, col_recv, across_send, across_recv,
):
    cols, short = staged.shape[:2]
    per_row = row_panel.shape[1]
    rows = cols // per_row
    pairs = rows * cols
    phases = cols // 2
    r, c = lax.axis_index("row"), lax.axis_index("col")

    points = x_ref.shape[0]
    upper = points // 2
    wide = 2 * points
    step = min(32, points)
    chunks = points // step

    def chunk(at):
        planes_of = pl.ds(at * step, step)
        return pltpu.make_async_copy(x_hbm.at[planes_of], x_ref.at[planes_of], chunk_loaded.at[at])

    operands = [
        (z_hbm, z_ref), (y_hbm, y_ref), (x_table_hbm, x_table_ref), (index_hbm, index_ref),
        (valence_band_hbm, valence_band), (conduction_band_hbm, conduction_band),
        (valence_energy_hbm, valence_energy), (conduction_energy_hbm, conduction_energy),
        (imag_freq_hbm, imag_freq),
    ]

    def load(at):
        source, target = operands[at]
        return pltpu.make_async_copy(source, target, loaded.at[at])

    load(0).start()
    chunk(0).start()
    load(1).start()
    for at in range(1, chunks):
        chunk(at).start()
    for at in range(2, len(operands)):
        load(at).start()

    def ahead(i):
        return lax.rem(r + i, rows)

    def onward(k):
        return lax.rem(c + k, cols)

    def loop(first, last, action):
        def body(at, carry):
            action(at)
            return carry

        lax.fori_loop(first, last, body, 0, unroll=last - first <= 8)

    barrier = pltpu.get_barrier_semaphore()

    def greet(at):
        pl.semaphore_signal(
            barrier, inc=1, device_id=(ahead(at // cols), onward(lax.rem(at, cols))),
            device_id_type=MESH)

    loop(1, pairs, greet)

    load(0).wait()
    load(1).wait()
    along_z, along_y = z_ref[...], y_ref[...]
    sign = jnp.where(lax.broadcasted_iota(jnp.int32, (points, wide), 1) < points, 1.0, -1.0)

    for at in range(chunks):
        chunk(at).wait()
    for at in range(chunks):
        start = at * step
        data = x_ref[start:start + step].reshape(step * points, points)
        lines = dot(jnp.concatenate([data, data], axis=1), along_z)
        high, low = split(lines)
        for pair in range(step // 2):
            blocks = []
            for side in range(2):
                lot = slice((2 * pair + side) * points, (2 * pair + side + 1) * points)
                blocks.append(jnp.concatenate([high[lot], low[lot], high[lot]], axis=0))
            result = dot(along_y, jnp.concatenate(blocks, axis=1))
            for side in range(2):
                part = result[:, side * wide:(side + 1) * wide]
                first = (start + 2 * pair + side) * points
                planes[first:first + points, :] = (
                    part[:points] + sign * pltpu.roll(part[points:], points, 1)
                )

    load(2).wait()
    along_x = x_table_ref[...]
    per_group = spectrum.shape[1] // LANES
    groups = points // 2 // per_group
    half_rows = groups * upper
    first_half = lax.broadcasted_iota(jnp.int32, (upper, wide), 1) < points

    for group in range(groups):

        @pl.loop(0, per_group, unroll=8)
        def _(place):
            base = 2 * (group * per_group + place)
            blocks = []
            for side in range(2):
                high, low = split(planes[pl.ds(base + side, points, stride=points), :])
                blocks.append(jnp.concatenate([high, low, high], axis=0))
            result = dot(along_x, jnp.concatenate(blocks, axis=1))
            even_cos, odd_cos = result[:upper, :wide], result[:upper, wide:]
            even_sin, odd_sin = result[upper:, :wide], result[upper:, wide:]

            def join(left, right, turn_left, turn_right):
                left = pltpu.roll(left, points, 1) if turn_left else left
                right = pltpu.roll(right, points, 1) if turn_right else right
                return jnp.where(first_half, left, right)

            real = join(even_cos, odd_cos, False, True) + join(even_sin, odd_sin, True, False)
            imag = join(even_sin, odd_sin, False, True) - join(even_cos, odd_cos, True, False)
            columns = pl.ds(pl.multiple_of(place * LANES, LANES), LANES)
            spectrum[group * upper:(group + 1) * upper, columns] = real.astype(jnp.bfloat16)
            spectrum[half_rows + group * upper:half_rows + (group + 1) * upper, columns] = (
                imag.astype(jnp.bfloat16)
            )

    depth = spectrum.shape[1]
    width = 256
    part = 256
    local = lax.broadcasted_iota(jnp.int32, (part, width), 0).astype(jnp.float32).astype(jnp.bfloat16)
    row_of = lax.broadcasted_iota(jnp.int32, (upper, width), 0)
    one = jnp.ones((part, width), jnp.bfloat16)
    zero = jnp.zeros((part, width), jnp.bfloat16)

    lines_per_step = width // LANES
    steps = short // lines_per_step
    load(3).wait()

    def select(own, step):
        line = step * lines_per_step
        start = pl.multiple_of((own * short + line) * LANES, width)
        index = index_ref[:, pl.ds(start, width)]
        column = index & (depth - 1)
        upper_part = index >> (depth.bit_length() - 1)
        block_of = column // part
        inside = (column % part).astype(jnp.float32).astype(jnp.bfloat16)
        hit = jnp.where(local == jnp.broadcast_to(inside, local.shape), one, zero)
        total = jnp.zeros((2 * half_rows, width), jnp.float32)
        for at in range(depth // part):
            flag = jnp.where(block_of == at, 1.0, 0.0).astype(jnp.bfloat16)
            total = total + dot(spectrum[:, at * part:(at + 1) * part], hit * flag)
        among = upper_part % groups
        mask = row_of == upper_part // groups

        def pick(half):
            kept = half[:upper]
            for group in range(1, groups):
                kept = jnp.where(among == group, half[group * upper:(group + 1) * upper], kept)
            return jnp.sum(jnp.where(mask, kept, 0.0), axis=0, keepdims=True)

        real, imag = pick(total[:half_rows]), pick(total[half_rows:])
        for side in range(lines_per_step):
            lanes = slice(side * LANES, (side + 1) * LANES)
            picked[pl.ds(line + side, 1), :] = real[:, lanes]
            picked[pl.ds(short + line + side, 1), :] = imag[:, lanes]

    def row_copy(own, k):
        return pltpu.make_async_remote_copy(
            src_ref=staged.at[own], dst_ref=row_panel.at[r * cols + c, lax.rem(own, per_row)],
            send_sem=row_send, recv_sem=row_recv,
            device_id=(own // per_row, onward(k)), device_id_type=MESH)

    parity = lax.rem(c, 2)

    def across(own, at):
        lot = lax.rem(own, per_row)
        return pltpu.make_async_remote_copy(
            src_ref=staged.at[own], dst_ref=row_panel.at[r * cols + c, lot],
            send_sem=across_send, recv_sem=across_recv.at[r, c // 2, lot],
            device_id=(own // per_row, 2 * at + parity), device_id_type=MESH)

    def other_core(own, at):
        return pltpu.make_async_remote_copy(
            src_ref=staged.at[own], dst_ref=row_panel.at[r * cols + c, lax.rem(own, per_row)],
            send_sem=row_send, recv_sem=row_recv,
            device_id=(own // per_row, 2 * at + 1 - parity), device_id_type=MESH)

    def pass_on(held):
        return pltpu.make_async_remote_copy(
            src_ref=held, dst_ref=held, send_sem=row_send, recv_sem=row_recv,
            device_id=(r, c + 1 - 2 * parity), device_id_type=MESH)

    def col_copy(own, i):
        return pltpu.make_async_remote_copy(
            src_ref=staged.at[own], dst_ref=col_panel.at[r * cols + c],
            send_sem=col_send, recv_sem=col_recv,
            device_id=(ahead(i), own), device_id_type=MESH)

    def is_direct(phase):
        return direct_last and phase == phases - 1

    def send_columns(own):
        loop(1, rows, lambda i: col_copy(own, i).start())

        @pl.when(own != c)
        def _():
            col_copy(own, 0).start()

        @pl.when(own == c)
        def _():
            col_panel[r * cols + c] = staged[own]

    def send_rows(own, phase):
        inside = own // per_row == r

        @pl.when(jnp.logical_not(inside))
        def _():
            loop(0, cols // 2, lambda at: across(own, at).start())
            if is_direct(phase):
                loop(0, cols // 2, lambda at: other_core(own, at).start())

        @pl.when(inside)
        def _():
            loop(1, cols, lambda k: row_copy(own, k).start())
            row_panel[r * cols + c, lax.rem(own, per_row)] = staged[own]

    def turn_of(row):
        return jnp.where(row < rows // 2, phases // 2, 0)

    def relay(phase, which):
        def one(i):
            source = ahead(i)
            own = lax.rem(phase + turn_of(source), phases)
            for side in range(2):
                group = own + side * phases
                mine = group // per_row == r
                if which == "early":
                    mine = jnp.logical_and(mine, source < r)
                elif which == "late":
                    mine = jnp.logical_and(mine, source > r)

                @pl.when(mine)
                def _():
                    lot = lax.rem(group, per_row)

                    def take(at):
                        held = row_panel.at[source * cols + 2 * at + parity, lot]
                        pltpu.make_async_copy(held, held, across_recv.at[source, at, lot]).wait()
                        if not is_direct(phase):
                            pass_on(held).start()

                    loop(0, cols // 2, take)

        loop(1, rows, one)

    for phase in range(phases):
        own = lax.rem(phase + turn_of(r), phases)

        @pl.loop(0, steps, unroll=min(8, steps))
        def _(step):
            select(own, step)

        for side in range(2):
            staged[own + side * phases] = picked[side * short:(side + 1) * short, :].astype(jnp.bfloat16)
        if phase == 0:
            pl.semaphore_wait(barrier, pairs - 1)
        for side in range(2):
            if phase < phases - 1:
                send_rows(own + side * phases, phase)
        for side in range(2):
            send_columns(own + side * phases)
        for side in range(2):
            if phase == phases - 1:
                send_rows(own + side * phases, phase)
        if phase >= 2:
            relay(phase - 2, "early")

    for at in range(4, len(operands)):
        load(at).wait()
    gap = lookup(conduction_band[...], conduction_energy[...]) - lookup(
        valence_band[...], valence_energy[...]
    )
    root = math.sqrt(gap.shape[0])
    for freq in range(weights.shape[1]):
        omega = imag_freq[:, freq:freq + 1]
        weights[:, freq:freq + 1] = -4.0 * gap / (gap * gap + omega * omega) / root

    for phase in range(phases):
        relay(phase, "late" if phase < phases - 2 else "all")

    for panel, count, sent, received in (
        (row_panel, cols - 1 + (rows - 1) * cols // 2, row_send, row_recv),
        (col_panel, pairs - 1, col_send, col_recv),
        (row_panel, (rows - 1) * cols // 2, across_send, None),
    ):
        part_of = panel.at[pl.ds(0, count)]
        if received is not None:
            pltpu.make_async_copy(part_of, part_of, received).wait()
        pltpu.make_async_copy(part_of, part_of, sent).wait()


def balanced(rows, cols):
    phases, per_row = cols // 2, cols // rows
    last = []
    for row in range(rows):
        own = (phases - 1 + (phases // 2 if row < rows // 2 else 0)) % phases
        last.append([own // per_row, (own + phases) // per_row])
    return all(
        sum(row in last[other] for other in range(rows) if other != row)
        == sum(target != row for target in last[row])
        for row in range(rows)
    )


def transform(product, pw_index, row_count, col_count, *bands):
    bands = [values.reshape(1, -1) for values in bands]
    points = product.shape[0]
    count = pw_index.shape[0]
    pairs = row_count * col_count
    lines = 2 * count // LANES
    tall, short = lines // row_count, lines // col_count
    tables = [jnp.asarray(table) for table in fourier_tables(points)]
    depth = 1024
    dma = pltpu.SemaphoreType.DMA
    operands = [product, pw_index.reshape(1, count), *tables, *bands]
    operands = [pltpu.with_memory_space_constraint(value, pltpu.HBM) for value in operands]
    return pl.pallas_call(
        functools.partial(transform_kernel, balanced(row_count, col_count)),
        out_shape=(
            pltpu.VMEM((pairs, tall // short, short, LANES), jnp.bfloat16),
            pltpu.VMEM((pairs, short, LANES), jnp.bfloat16),
            pltpu.VMEM((bands[0].shape[1], bands[-1].shape[1]), jnp.float32),
        ),
        in_specs=[pl.BlockSpec(memory_space=pltpu.HBM)] * len(operands),
        out_specs=(pl.BlockSpec(memory_space=pltpu.VMEM),) * 3,
        scratch_shapes=[pltpu.VMEM(value.shape, value.dtype) for value in operands] + [
            pltpu.VMEM((points * points, 2 * points), jnp.float32),
            pltpu.VMEM((points**3 // depth, depth), jnp.bfloat16),
            pltpu.VMEM((2 * short, LANES), jnp.float32),
            pltpu.VMEM((col_count, short, LANES), jnp.bfloat16),
            dma((len(operands) - 1,)), dma((points // min(32, points),)),
            dma, dma, dma, dma, dma, dma((row_count, col_count // 2, tall // short)),
        ],
        compiler_params=pltpu.CompilerParams(collective_id=0, has_side_effects=True),
        name="spectrum",
    )(*operands)


def product_kernel(row_ref, col_ref, weight_ref, out_ref, row_lines, col_lines, left, right, ring, sems):
    pairs = row_ref.shape[0]
    freq_count, row_width, _ = out_ref.shape
    slots, height = ring.shape[0], ring.shape[1]
    wide = [
        jnp.broadcast_to(weight_ref[:, freq:freq + 1], (pairs, LANES)) for freq in range(freq_count)
    ]
    stacked = len(col_ref.shape) == 3
    col_blocks = col_ref.shape[1] if stacked else col_ref.shape[1] // LANES
    if stacked:
        col_lines[...] = col_ref[...].astype(jnp.float32).reshape(col_lines.shape)
    if len(row_ref.shape) == 3:
        row_lines[...] = row_ref[...].astype(jnp.float32).reshape(row_lines.shape)

    def weigh(freq):
        for block in range(col_blocks):
            lanes = slice(block * LANES, (block + 1) * LANES)
            if stacked:
                values = col_lines[pl.ds(block, pairs, stride=col_blocks), :]
            else:
                values = col_ref[:, lanes].astype(jnp.float32)
            right[freq, :, lanes] = (values * wide[freq]).astype(jnp.bfloat16)

    def turn(step, part):
        block = step * (height // LANES) + part
        if len(row_ref.shape) == 3:
            values = row_lines[pl.ds(block, pairs, stride=row_ref.shape[1]), :]
        else:
            values = row_ref[:, pl.ds(pl.multiple_of(block * LANES, LANES), LANES)]
            values = values.astype(jnp.float32)
        left[part * LANES:(part + 1) * LANES, :] = values.T.astype(jnp.bfloat16)

    steps = row_width // height

    def write(slot, freq, step):
        rows = pl.ds(pl.multiple_of(step * height, height), height)
        return pltpu.make_async_copy(ring.at[slot], out_ref.at[freq, rows], sems.at[slot])

    lead = LANES // 4
    for freq in range(freq_count):
        weigh(freq)
        for first in range(0, height, lead):
            if freq == 0 and first % LANES == 0:
                turn(0, first // LANES)
            rows = slice(first, first + lead)
            ring[freq, rows] = dot(left[rows], right[freq])
            pltpu.make_async_copy(
                ring.at[freq, rows], out_ref.at[freq, rows], sems.at[freq]
            ).start()

    @pl.loop(1, steps)
    def _(step):
        for part in range(height // LANES):
            turn(step, part)
        panel = left[...]
        for freq in range(freq_count):
            unit = step * freq_count + freq
            slot = lax.rem(unit, slots)

            @pl.when(unit >= slots)
            def _():
                write(slot, freq, step).wait()

            ring[slot] = dot(panel, right[freq])
            write(slot, freq, step).start()

    for slot in range(min(slots, steps * freq_count)):
        write(slot, 0, 0).wait()


def product(row_panel, col_panel, weights):
    pairs, freq_count = weights.shape
    row_panel = row_panel.reshape(pairs, -1, LANES)
    row_width = row_panel.shape[1] * LANES
    col_width = col_panel.shape[1] * LANES
    panels = []
    lines = []
    for panel in (row_panel, col_panel):
        height = panel.shape[1]
        if height % 16 == 0:
            panels.append(pltpu.with_memory_space_constraint(panel, pltpu.VMEM))
            lines.append(pltpu.VMEM((pairs * height, LANES), jnp.float32))
        else:
            panels.append(panel.reshape(pairs, height * LANES))
            lines.append(pltpu.VMEM((8, LANES), jnp.float32))
    block = min(256, row_width)
    slots = max(4, freq_count)
    whole = pl.BlockSpec(memory_space=pltpu.VMEM)
    return pl.pallas_call(
        product_kernel,
        out_shape=jax.ShapeDtypeStruct((freq_count, row_width, col_width), jnp.float32),
        in_specs=[whole, whole, whole],
        out_specs=pl.BlockSpec(memory_space=pl.ANY),
        scratch_shapes=lines + [
            pltpu.VMEM((block, pairs), jnp.bfloat16),
            pltpu.VMEM((freq_count, pairs, col_width), jnp.bfloat16),
            pltpu.VMEM((slots, block, col_width), jnp.float32),
            pltpu.SemaphoreType.DMA((slots,)),
        ],
        name="product",
    )(*panels, pltpu.with_memory_space_constraint(weights, pltpu.VMEM))


def shards(
    pair_products,
    pw_index,
    valence_band,
    conduction_band,
    valence_energy,
    conduction_energy,
    imag_freq,
):
    rows, cols = lax.axis_size("row"), lax.axis_size("col")
    row_panel, col_panel, weights = transform(
        pair_products[0], pw_index, rows, cols,
        valence_band, conduction_band, valence_energy, conduction_energy, imag_freq,
    )
    return product(row_panel, col_panel, weights)


def solution(mesh):
    in_specs = (P(("row", "col"), None, None, None), P(), P(), P(), P(), P(), P())
    out_specs = P(None, "row", "col")
    return jax.shard_map(shards, mesh=mesh, in_specs=in_specs, out_specs=out_specs, check_vma=False)
```
